32 devices in a mesh: dp: 8 (over y, x, core), tensor: 4 (over z).
Axes of the slice: x: 2, y: 2, z: 4, core: 2. Of those that a mesh axis runs over, the one named last changes fastest.
Arguments:
- block_input: bfloat16 [4096, 768], P(('dp', 'tensor')), may hold values from -6 to 6
- seq_lengths: int32 [8, 4], P('dp'), may hold values from 0 to 512, as said below
- w_qkv: bfloat16 [768, 2304], P(None, 'tensor'), may hold values from -3 to 3
- b_query: float32 [768], P('tensor'), may hold values from -3 to 3
- b_value: float32 [768], P('tensor'), may hold values from -3 to 3
- w_out: bfloat16 [768, 768], P('tensor'), may hold values from -1 to 1
- b_out: float32 [768], replicated, may hold values from -3 to 3
- w_up: bfloat16 [768, 3072], P(None, 'tensor'), may hold values from -0.21875 to 0.21875
- b_up: float32 [3072], P('tensor'), may hold values from -3 to 3
- w_down: bfloat16 [3072, 768], P('tensor'), may hold values from -0.109375 to 0.109375
- b_down: float32 [768], replicated, may hold values from -3 to 3
- first_norm_gain: float32 [768], replicated, may hold values from 0.1 to 1.9
- first_norm_bias: float32 [768], replicated, may hold values from -2 to 2
- second_norm_gain: float32 [768], replicated, may hold values from 0.1 to 1.9
- second_norm_bias: float32 [768], replicated, may hold values from -2 to 2
- cotangent: bfloat16 [4096, 768], P(('dp', 'tensor')), may hold values from -6 to 6
Outputs:
- block_output: bfloat16 [4096, 768], P(('dp', 'tensor'))
- grad_input: float32 [4096, 768], P(('dp', 'tensor'))
- grad_w_qkv: float32 [768, 2304], P(None, 'tensor')
- grad_b_query: float32 [768], P('tensor')
- grad_b_value: float32 [768], P('tensor')
- grad_w_out: float32 [768, 768], P('tensor')
- grad_b_out: float32 [768], replicated
- grad_w_up: float32 [768, 3072], P(None, 'tensor')
- grad_b_up: float32 [3072], P('tensor')
- grad_w_down: float32 [3072, 768], P('tensor')
- grad_b_down: float32 [768], replicated
- first_norm_gain_gradient: float32 [768], replicated
- first_norm_bias_gradient: float32 [768], replicated
- second_norm_gain_gradient: float32 [768], replicated
- second_norm_bias_gradient: float32 [768], replicated
The draws below stay inside these ranges and needn't reach their ends.
Inputs may be any that keep to these rules, and one draw needn't show every extreme that they name: `seq_lengths`: row g lists the lengths of the sequences packed one after another from slot 0 into the 512 slots of group g; a row sums to at most 512, some entries may be 0, and some row fills all its slots.
All inputs are finite; a program needn't handle non-finite values.
Results may differ from the reference program's by a relative error of at most 0.012.
Values may be sent and summed in bfloat16 or wider, within the bound.
No kernel may reach another device: no remote copies, remote signals or barrier semaphores. Data moves between devices by JAX's collectives and lax.ppermute only.
A program may use at most 64 MiB of HBM per device.

```python
import math
import jax
import jax.numpy as jnp
from jax import lax

D = 768
HEADS = 12
FF = 3072
TOK_DEV = 512
SEQ_DEV = 4
HD = 64
QBLOCK = 512
GROUPS = 8
TOKENS = 4096


def draw_seq_lengths(key, part):
    key_total, key_full, key_cuts = jax.random.split(key, 3)
    row_totals = jax.random.randint(key_total, (GROUPS,), TOK_DEV // 4, TOK_DEV + 1).astype(jnp.int32)
    full_row = jax.random.randint(key_full, (), 0, GROUPS).astype(jnp.int32)
    row_index = jnp.arange(GROUPS, dtype=jnp.int32)
    cut_points = jax.random.randint(key_cuts, (GROUPS, SEQ_DEV - 1), 0, TOK_DEV + 1).astype(jnp.int32)
    cut_points = jnp.sort(cut_points * row_totals[:, None] // TOK_DEV, axis=1).astype(jnp.int32)
    bounds = jnp.concatenate([jnp.zeros((GROUPS, 1), jnp.int32), cut_points, row_totals[:, None]], axis=1)
    lengths = bounds[:, 1:] - bounds[:, :-1]
    single = jnp.where(jnp.arange(SEQ_DEV, dtype=jnp.int32) == 0, TOK_DEV, 0).astype(jnp.int32)
    return jnp.where((row_index == full_row)[:, None], single[None, :], lengths).astype(jnp.int32)


def draw_w_qkv(key, part):
    key_base = jax.random.fold_in(key, 0)
    weights = jax.random.truncated_normal(key_base, -3.5, 3.5, (D, HEADS, 3, HD), jnp.float32) * D ** (-0.5)
    return weights.reshape(D, 3 * D).astype(jnp.bfloat16)


def strengthened(values, rng, source, target, blocks, factor):
    owner, partner = [(jnp.arange(values.shape[dim]) // (values.shape[dim] // blocks)).reshape([-1 if axis == dim else 1 for axis in range(values.ndim)]) for dim in (source, target)]
    chosen = jax.random.permutation(rng, blocks)[partner]
    strong = (owner == chosen) | (owner == (partner + blocks // 2) % blocks)
    return jnp.where(strong, factor * values, values)


def level_of(stream_key, shape, cuts, low, largest):
    def one(position, blocks):
        heights = jax.random.uniform(jax.random.fold_in(jax.random.fold_in(stream_key, 6), position), (blocks,), jnp.float32, low / len(cuts), largest / len(cuts))
        return jnp.repeat(jnp.exp(heights), shape[position] // blocks).reshape((-1,) + (1,) * (len(shape) - position - 1))

    level = one(*cuts[0])
    for cut in cuts[1:]:
        level = level * one(*cut)
    return level


def gaussian(own_key, extent, width, reach, shards=(), held_as=jnp.bfloat16):
    entries = width * jax.random.normal(own_key, extent, jnp.float32)
    if shards:
        entries = entries * level_of(own_key, extent, shards, -0.22, 0.18)
    return jnp.clip(entries, -reach, reach).astype(held_as)


def heavy_noise(own_key, dims, scale, reach, cuts, heavy, kind=jnp.bfloat16):
    result = scale * jax.random.normal(own_key, dims, jnp.float32)
    if cuts:
        result = result * level_of(own_key, dims, cuts, -0.22, 0.18)
    return jnp.clip(strengthened(result, jax.random.fold_in(own_key, 3), *heavy), -reach, reach).astype(kind)


def setup_inputs(seed: int = 0) -> dict:
    key_of = jax.random.split(jax.random.key(seed), 17)
    block_input = gaussian(key_of[0], (TOKENS, D), 1.0, 6.0, ((0, 32),))
    seq_lengths = draw_seq_lengths(jax.random.fold_in(key_of[16], 71), 0)
    w_qkv = draw_w_qkv(jax.random.fold_in(key_of[16], 71), 0)
    b_query = gaussian(key_of[3], (D,), 0.5, 3.0, ((0, 4),), jnp.float32)
    b_value = gaussian(key_of[4], (D,), 0.5, 3.0, ((0, 4),), jnp.float32)
    w_out = gaussian(key_of[5], (D, D), 32 ** -0.5, 1.0, ((0, 4),))
    b_out = gaussian(key_of[6], (D,), 0.5, 3.0, (), jnp.float32)
    w_up = gaussian(key_of[7], (D, FF), D ** -0.5, 0.21875, ((1, 4),))
    b_up = gaussian(key_of[8], (FF,), 0.5, 3.0, ((0, 4),), jnp.float32)
    w_down = gaussian(key_of[9], (FF, D), FF ** -0.5, 0.109375, ((0, 4),))
    b_down = gaussian(key_of[10], (D,), 0.5, 3.0, (), jnp.float32)
    first_norm_gain = jnp.clip(1.0 + 0.18 * jax.random.normal(key_of[11], (D,), jnp.float32), 0.1, 1.9)
    first_norm_bias = gaussian(key_of[12], (D,), 0.3, 2.0, (), jnp.float32)
    second_norm_gain = jnp.clip(1.0 + 0.18 * jax.random.normal(key_of[13], (D,), jnp.float32), 0.1, 1.9)
    second_norm_bias = gaussian(key_of[14], (D,), 0.3, 2.0, (), jnp.float32)
    cotangent = heavy_noise(key_of[15], (TOKENS, D), 1.0, 6.0, ((0, 32),), (0, 1, 32, 2.75))
    return dict(block_input=block_input, seq_lengths=seq_lengths, w_qkv=w_qkv, b_query=b_query, b_value=b_value, w_out=w_out, b_out=b_out, w_up=w_up, b_up=b_up, w_down=w_down, b_down=b_down, first_norm_gain=first_norm_gain, first_norm_bias=first_norm_bias, second_norm_gain=second_norm_gain, second_norm_bias=second_norm_bias, cotangent=cotangent)


GELU_COEF = 0.7978845608028654
GELU_CUBE = 0.044715
NORM_EPS = 1e-05

def gelu_tanh(values):
    inner_arg = GELU_COEF * (values + GELU_CUBE * values * values * values)
    return 0.5 * values * (1.0 + jnp.tanh(inner_arg))

def gelu_slope(values):
    tangent = jnp.tanh(GELU_COEF * (values + GELU_CUBE * values * values * values))
    return 0.5 * (1.0 + tangent) + 0.5 * values * (1.0 - tangent * tangent) * GELU_COEF * (1.0 + 3.0 * GELU_CUBE * values * values)

def layer_normalize(values, gain, bias_vec):
    row_mean = lax.optimization_barrier(jnp.mean(values, axis=-1, keepdims=True))
    centred = values - row_mean
    rstd_row = lax.rsqrt(lax.optimization_barrier(jnp.mean(centred * centred, axis=-1, keepdims=True)) + NORM_EPS)
    normed = centred * rstd_row
    return ((normed * gain + bias_vec).astype(jnp.bfloat16), normed, rstd_row)

def layer_normalize_backward(grad_normed, normed, rstd_row, gain):
    scaled = grad_normed * gain
    inner_mean = lax.optimization_barrier(jnp.mean(scaled * normed, axis=-1, keepdims=True))
    grad_rows = rstd_row * (scaled - lax.optimization_barrier(jnp.mean(scaled, axis=-1, keepdims=True)) - normed * inner_mean)
    return (grad_rows, lax.optimization_barrier(jnp.sum(grad_normed * normed, axis=0)), lax.optimization_barrier(jnp.sum(grad_normed, axis=0)))

def slot_segments(lengths_row, slot_ids):
    seq_ends = jnp.cumsum(lengths_row).astype(jnp.int32)
    segment = lax.optimization_barrier(jnp.sum((slot_ids[:, None] >= seq_ends[None, :]).astype(jnp.int32), axis=1))
    valid_slot = (slot_ids < seq_ends[-1]).astype(jnp.float32)
    return (segment, valid_slot)

def block_scores(query_block, key_rows, segment, slot_ids, block_start, block_rows):
    scale = 1.0 / math.sqrt(HD)
    seg_block = segment[block_start:block_start + block_rows]
    slot_block = slot_ids[block_start:block_start + block_rows]
    allowed = (seg_block[:, None] == segment[None, :]) & (slot_ids[None, :] <= slot_block[:, None])
    scores = jnp.einsum('qhe,khe->hqk', query_block.astype(jnp.float32), key_rows.astype(jnp.float32)) * scale
    return jnp.where(allowed[None, :, :], scores, -jnp.inf)

def attend_forward(queries, key_rows, values, segment, slot_ids):
    outputs = []
    totals = []
    for block_start in range(0, TOK_DEV, QBLOCK):
        scores = block_scores(queries[block_start:block_start + QBLOCK], key_rows, segment, slot_ids, block_start, QBLOCK)
        row_top = lax.optimization_barrier(jnp.max(scores, axis=-1, keepdims=True))
        log_total = row_top + jnp.log(lax.optimization_barrier(jnp.sum(jnp.exp(scores - row_top), axis=-1, keepdims=True)))
        prob_bf = jnp.exp(scores - log_total).astype(jnp.bfloat16)
        outputs.append(jnp.einsum('hqk,khe->qhe', prob_bf.astype(jnp.float32), values.astype(jnp.float32)).astype(jnp.bfloat16))
        totals.append(log_total)
    return (jnp.concatenate(outputs, axis=0), totals)

def attend_backward(queries, key_rows, values, attended, grad_att, totals, segment, slot_ids):
    scale = 1.0 / math.sqrt(HD)
    grad_query_list = []
    grad_keys = jnp.zeros(key_rows.shape, jnp.float32)
    grad_values = jnp.zeros(values.shape, jnp.float32)
    for block_index in range(TOK_DEV // QBLOCK):
        block_start = block_index * QBLOCK
        query_block = queries[block_start:block_start + QBLOCK]
        scores = block_scores(query_block, key_rows, segment, slot_ids, block_start, QBLOCK)
        prob_full = jnp.exp(scores - totals[block_index])
        prob_bf = prob_full.astype(jnp.bfloat16)
        grad_block = grad_att[block_start:block_start + QBLOCK]
        grad_values = grad_values + jnp.einsum('hqk,qhe->khe', prob_bf.astype(jnp.float32), grad_block.astype(jnp.float32))
        grad_probs = jnp.einsum('qhe,khe->hqk', grad_block.astype(jnp.float32), values.astype(jnp.float32))
        row_delta = lax.optimization_barrier(jnp.sum(grad_block.astype(jnp.float32) * attended[block_start:block_start + QBLOCK].astype(jnp.float32), axis=-1))
        grad_scores = (prob_full * (grad_probs - jnp.transpose(row_delta)[:, :, None]) * scale).astype(jnp.bfloat16)
        grad_query_list.append(jnp.einsum('hqk,khe->qhe', grad_scores.astype(jnp.float32), key_rows.astype(jnp.float32)))
        grad_keys = grad_keys + jnp.einsum('hqk,qhe->khe', grad_scores.astype(jnp.float32), query_block.astype(jnp.float32))
    return (jnp.concatenate(grad_query_list, axis=0), grad_keys, grad_values)

def layer_group(params, input_rows, cot_rows, lengths_row):
    w_qkv, b_query, b_value, w_out, b_out, w_up, b_up, w_down, b_down, first_norm_gain, first_norm_bias, second_norm_gain, second_norm_bias = params
    slot_ids = jnp.arange(TOK_DEV, dtype=jnp.int32)
    segment, valid_slot = slot_segments(lengths_row, slot_ids)
    valid_col = valid_slot[:, None]
    input_as_float = input_rows.astype(jnp.float32)
    first_normalized, first_standardized, first_inverse_deviation = layer_normalize(input_as_float, first_norm_gain, first_norm_bias)
    joined_rows = jnp.dot(first_normalized, w_qkv, preferred_element_type=jnp.float32).reshape(TOK_DEV, HEADS, 3, HD)
    queries = (joined_rows[:, :, 0] + b_query.reshape(HEADS, HD)).astype(jnp.bfloat16)
    key_rows = joined_rows[:, :, 1].astype(jnp.bfloat16)
    values = (joined_rows[:, :, 2] + b_value.reshape(HEADS, HD)).astype(jnp.bfloat16)
    attended, totals = attend_forward(queries, key_rows, values, segment, slot_ids)
    attended_flat = attended.reshape(TOK_DEV, D)
    residual_stream_rows = input_as_float + jnp.dot(attended_flat, w_out, preferred_element_type=jnp.float32) + b_out
    second_normalized, second_standardized, second_inverse_deviation = layer_normalize(residual_stream_rows, second_norm_gain, second_norm_bias)
    pre_act = jnp.dot(second_normalized, w_up, preferred_element_type=jnp.float32) + b_up
    activation = gelu_tanh(pre_act).astype(jnp.bfloat16)
    final_rows = residual_stream_rows + jnp.dot(activation, w_down, preferred_element_type=jnp.float32) + b_down
    output_rows = (final_rows * valid_col).astype(jnp.bfloat16)
    grad_final = cot_rows.astype(jnp.float32) * valid_col
    grad_final_bf = grad_final.astype(jnp.bfloat16)
    grad_w_down = jnp.dot(activation.T, grad_final_bf, preferred_element_type=jnp.float32)
    grad_b_down = lax.optimization_barrier(jnp.sum(grad_final, axis=0))
    grad_pre = jnp.dot(grad_final_bf, w_down.T, preferred_element_type=jnp.float32) * gelu_slope(pre_act)
    grad_pre_bf = grad_pre.astype(jnp.bfloat16)
    grad_w_up = jnp.dot(second_normalized.T, grad_pre_bf, preferred_element_type=jnp.float32)
    grad_b_up = lax.optimization_barrier(jnp.sum(grad_pre, axis=0))
    second_normalized_gradient = jnp.dot(grad_pre_bf, w_up.T, preferred_element_type=jnp.float32)
    second_norm_backward, second_norm_gain_gradient, second_norm_bias_gradient = layer_normalize_backward(second_normalized_gradient, second_standardized, second_inverse_deviation, second_norm_gain)
    grad_residual = grad_final + second_norm_backward
    grad_residual_bf = grad_residual.astype(jnp.bfloat16)
    grad_w_out = jnp.dot(attended_flat.T, grad_residual_bf, preferred_element_type=jnp.float32)
    grad_b_out = lax.optimization_barrier(jnp.sum(grad_residual, axis=0))
    grad_att = jnp.dot(grad_residual_bf, w_out.T, preferred_element_type=jnp.float32).astype(jnp.bfloat16).reshape(TOK_DEV, HEADS, HD)
    grad_queries, grad_keys, grad_values = attend_backward(queries, key_rows, values, attended, grad_att, totals, segment, slot_ids)
    grad_b_query = lax.optimization_barrier(jnp.sum(grad_queries, axis=0)).reshape(D)
    grad_b_value = lax.optimization_barrier(jnp.sum(grad_values, axis=0)).reshape(D)
    grad_joined = jnp.stack([grad_queries.astype(jnp.bfloat16), grad_keys.astype(jnp.bfloat16), grad_values.astype(jnp.bfloat16)], axis=2).reshape(TOK_DEV, 3 * D)
    grad_w_qkv = jnp.dot(first_normalized.T, grad_joined, preferred_element_type=jnp.float32)
    first_normalized_gradient = jnp.dot(grad_joined, w_qkv.T, preferred_element_type=jnp.float32)
    first_norm_backward, first_norm_gain_gradient, first_norm_bias_gradient = layer_normalize_backward(first_normalized_gradient, first_standardized, first_inverse_deviation, first_norm_gain)
    grad_rows = grad_residual + first_norm_backward
    grads = (grad_w_qkv, grad_b_query, grad_b_value, grad_w_out, grad_b_out, grad_w_up, grad_b_up, grad_w_down, grad_b_down, first_norm_gain_gradient, first_norm_bias_gradient, second_norm_gain_gradient, second_norm_bias_gradient)
    return (output_rows, grad_rows, grads)

def reference(block_input, seq_lengths, w_qkv, b_query, b_value, w_out, b_out, w_up, b_up, w_down, b_down, first_norm_gain, first_norm_bias, second_norm_gain, second_norm_bias, cotangent):
    params = (w_qkv, b_query, b_value, w_out, b_out, w_up, b_up, w_down, b_down, first_norm_gain, first_norm_bias, second_norm_gain, second_norm_bias)
    grouped_input = block_input.reshape(GROUPS, TOK_DEV, D)
    grouped_cot = cotangent.reshape(GROUPS, TOK_DEV, D)
    zero_grads = tuple((jnp.zeros(param.shape, jnp.float32) for param in params))

    def group_pass(running, inputs):
        input_rows, cot_rows, lengths_row = inputs
        output_rows, grad_rows, grads = layer_group(params, input_rows, cot_rows, lengths_row)
        running = tuple((total + grad for total, grad in zip(running, grads)))
        return (running, (output_rows, grad_rows))
    running, (outputs, grad_inputs) = lax.scan(group_pass, zero_grads, (grouped_input, grouped_cot, seq_lengths))
    grad_w_qkv, grad_b_query, grad_b_value, grad_w_out, grad_b_out, grad_w_up, grad_b_up, grad_w_down, grad_b_down, first_norm_gain_gradient, first_norm_bias_gradient, second_norm_gain_gradient, second_norm_bias_gradient = running
    return (outputs.reshape(TOKENS, D), grad_inputs.reshape(TOKENS, D), grad_w_qkv, grad_b_query, grad_b_value, grad_w_out, grad_b_out, grad_w_up, grad_b_up, grad_w_down, grad_b_down, first_norm_gain_gradient, first_norm_bias_gradient, second_norm_gain_gradient, second_norm_bias_gradient)
```

```python
import math

import jax
import jax.numpy as jnp
from jax import lax
from jax.sharding import PartitionSpec as P

HD = 64
GELU_COEF = 0.7978845608028654
GELU_CUBE = 0.044715
NORM_EPS = 1e-05
BF = jnp.bfloat16
F32 = jnp.float32


def dot(left, right, dims):
    return lax.dot_general(left, right, (dims, ((), ())), preferred_element_type=F32)


def swap(x, axis, mask):
    n = lax.axis_size(axis)
    return lax.ppermute(x, axis, [(i, i ^ mask) for i in range(n)])


def gelu_parts(values):
    tangent = jnp.tanh(GELU_COEF * (values + GELU_CUBE * values * values * values))
    act = 0.5 * values * (1.0 + tangent)
    slope = 0.5 * (1.0 + tangent) + 0.5 * values * (1.0 - tangent * tangent) * GELU_COEF * (
        1.0 + 3.0 * GELU_CUBE * values * values
    )
    return act, slope


def standardize(values):
    centred = values - jnp.mean(values, axis=-1, keepdims=True)
    rstd = lax.rsqrt(jnp.mean(centred * centred, axis=-1, keepdims=True) + NORM_EPS)
    return centred * rstd, rstd


def norm_backward(grad_normed, xhat, rstd, gain):
    scaled = grad_normed * gain
    inner = jnp.mean(scaled * xhat, axis=-1, keepdims=True)
    return rstd * (scaled - jnp.mean(scaled, axis=-1, keepdims=True) - xhat * inner)


def z_masks():
    return range(1, lax.axis_size("tensor"))


def plane_size():
    return min(8, lax.axis_size("dp"))


def gather_z(x):
    return [x] + [swap(x, "tensor", m) for m in z_masks()]


def exchange_z(blocks):
    return [blocks[0]] + [swap(blocks[m], "tensor", m) for m in z_masks()]


def gather_plane(x):
    mine = jnp.concatenate([x] + [swap(x, "dp", m) for m in range(2, plane_size(), 2)], axis=0)
    return jnp.concatenate([mine, swap(mine, "dp", 1)], axis=0)


def plane_order():
    n = plane_size()
    return list(range(0, n, 2)) + list(range(1, n, 2))


def reduce_plane(parts):
    n = plane_size()
    half = parts.shape[0] // 2
    rows = parts.shape[0] // n
    mine = parts[:half] + swap(parts[half:].astype(BF), "dp", 1).astype(F32)
    total = mine[:rows]
    for k in range(1, n // 2):
        total = total + swap(mine[k * rows : (k + 1) * rows].astype(BF), "dp", 2 * k).astype(F32)
    return total


def sum_beyond_plane(x):
    mask = plane_size()
    while mask < lax.axis_size("dp"):
        x = x + swap(x, "dp", mask)
        mask *= 2
    return x


def sum_dp(x):
    mask = 1
    while mask < lax.axis_size("dp"):
        x = x + swap(x, "dp", mask)
        mask *= 2
    return x


def sum_z(x):
    mask = 1
    while mask < lax.axis_size("tensor"):
        x = x + swap(x, "tensor", mask)
        mask *= 2
    return x


def plane_permutation(outer, sub, inner):
    n = outer * sub * inner
    p = lax.axis_index("dp") % sub
    nat = lax.broadcasted_iota(jnp.int32, (n, n), 0)
    per = lax.broadcasted_iota(jnp.int32, (n, n), 1)
    k = per // (outer * inner)
    half = sub // 2
    mask = jnp.where(k < half, 2 * k, 2 * (k - half) + 1)
    j = p ^ mask
    o = (per // inner) % outer
    i = per % inner
    return (nat == (o * sub + j) * inner + i).astype(BF)


def plane_slice(size, sub):
    width = size // sub
    p = lax.axis_index("dp") % sub
    row = lax.broadcasted_iota(jnp.int32, (size, width), 0)
    col = lax.broadcasted_iota(jnp.int32, (size, width), 1)
    return (row == p * width + col).astype(BF)


def masked_scores(queries, keys, allowed):
    scores = jnp.einsum("qhe,khe->hqk", queries, keys, preferred_element_type=F32)
    return jnp.where(allowed[None], scores * (1.0 / math.sqrt(HD)), -jnp.inf)


def attend_forward(queries, keys, values, allowed):
    scores = masked_scores(queries, keys, allowed)
    top = jnp.max(scores, axis=-1, keepdims=True)
    log_total = top + jnp.log(jnp.sum(jnp.exp(scores - top), axis=-1, keepdims=True))
    probs = jnp.exp(scores - log_total).astype(BF)
    attended = jnp.einsum("hqk,khe->qhe", probs, values, preferred_element_type=F32).astype(BF)
    return attended, log_total


def attend_backward(queries, keys, values, attended, grad_att, log_total, allowed):
    scores = masked_scores(queries, keys, allowed)
    prob_full = jnp.exp(scores - log_total)
    probs = prob_full.astype(BF)
    grad_values = jnp.einsum("hqk,qhe->khe", probs, grad_att, preferred_element_type=F32)
    grad_probs = jnp.einsum("qhe,khe->hqk", grad_att, values, preferred_element_type=F32)
    delta = jnp.sum(grad_att.astype(F32) * attended.astype(F32), axis=-1)
    grad_scores = (
        prob_full * (grad_probs - jnp.transpose(delta)[:, :, None]) * (1.0 / math.sqrt(HD))
    ).astype(BF)
    grad_queries = jnp.einsum("hqk,khe->qhe", grad_scores, keys, preferred_element_type=F32)
    grad_keys = jnp.einsum("hqk,qhe->khe", grad_scores, queries, preferred_element_type=F32)
    return grad_queries, grad_keys, grad_values


def local(
    block_input,
    seq_lengths,
    w_qkv,
    b_query,
    b_value,
    w_out,
    b_out,
    w_up,
    b_up,
    w_down,
    b_down,
    first_norm_gain,
    first_norm_bias,
    second_norm_gain,
    second_norm_bias,
    cotangent,
):
    own, width = block_input.shape
    nz = lax.axis_size("tensor")
    sub = plane_size()
    t = lax.axis_index("tensor")
    group_rows = own * nz
    heads = w_out.shape[0] // HD
    head_cols = heads * HD

    row = jnp.arange(group_rows, dtype=jnp.int32)
    slots = ((row // own) ^ t) * own + row % own
    seq_ends = jnp.cumsum(seq_lengths[0])
    segment = jnp.sum((slots[:, None] >= seq_ends[None, :]).astype(jnp.int32), axis=1)
    allowed = (segment[:, None] == segment[None, :]) & (slots[None, :] <= slots[:, None])
    valid_col = (slots[:own] < seq_ends[-1]).astype(F32)[:, None]

    input_blocks = gather_z(block_input)
    grad_final = cotangent.astype(F32) * valid_col
    cot_all = gather_plane(grad_final.astype(BF))

    pick = plane_slice(w_up.shape[1], sub)
    up_part = dot(pick, w_up, ((0,), (1,))).astype(BF)
    down_part = dot(pick, w_down, ((0,), (0,))).astype(BF)
    units = up_part.shape[0]
    p = lax.axis_index("dp") % sub
    bias_part = lax.dynamic_slice_in_dim(b_up, p * units, units, 0)[None]
    out_part = dot(plane_slice(head_cols, sub), w_out, ((0,), (0,))).astype(BF)
    out_z = jnp.concatenate(gather_z(out_part), axis=0)
    out_stack = gather_plane(out_z)
    ffn_blocks = gather_z(jnp.concatenate([up_part, down_part], axis=0))
    bias_blocks = gather_z(bias_part)
    up_t = jnp.concatenate([b[:units] for b in ffn_blocks], axis=0)
    down = jnp.concatenate([b[units:] for b in ffn_blocks], axis=0)
    bias_up = jnp.concatenate(bias_blocks, axis=1)
    out_perm = plane_permutation(nz, sub, head_cols // sub)
    out_full = dot(out_perm, out_stack, ((1,), (0,))).astype(BF)

    input_all = jnp.concatenate(input_blocks, axis=0).astype(F32)
    xhat_all, rstd_all = standardize(input_all)
    rows_one = (xhat_all * first_norm_gain + first_norm_bias).astype(BF)
    joined = dot(rows_one, w_qkv, ((1,), (0,))).reshape(group_rows, heads, 3, HD)
    queries = (joined[:, :, 0] + b_query.reshape(heads, HD)).astype(BF)
    keys = joined[:, :, 1].astype(BF)
    values = (joined[:, :, 2] + b_value.reshape(heads, HD)).astype(BF)
    attended, log_total = attend_forward(queries, keys, values, allowed)
    attended_flat = attended.reshape(group_rows, head_cols)
    attended_rows = jnp.concatenate(
        exchange_z([attended_flat[m * own : (m + 1) * own] for m in range(nz)]), axis=1
    )

    residual = input_all[:own] + dot(attended_rows, out_full, ((1,), (0,))) + b_out
    xhat_two, rstd_two = standardize(residual)
    normed_two = (xhat_two * second_norm_gain + second_norm_bias).astype(BF)
    rows_two = gather_plane(normed_two)

    pre_act = dot(rows_two, up_t, ((1,), (1,))) + bias_up
    act, slope = gelu_parts(pre_act)
    activation = act.astype(BF)
    grad_pre = dot(cot_all, down, ((1,), (1,))) * slope
    grad_pre_bf = grad_pre.astype(BF)
    second_grad = reduce_plane(dot(grad_pre_bf, up_t, ((1,), (0,))))
    mlp_rows = reduce_plane(dot(activation, down, ((1,), (0,))))
    block_output = ((residual + mlp_rows + b_down) * valid_col).astype(BF)
    up_grad = dot(grad_pre_bf, rows_two, ((0,), (0,)))
    down_grad = dot(activation, cot_all, ((0,), (0,)))
    bias_up_grad = jnp.sum(grad_pre, axis=0)

    back_two = norm_backward(second_grad, xhat_two, rstd_two, second_norm_gain)
    grad_residual = grad_final + back_two
    grad_residual_bf = grad_residual.astype(BF)
    grad_att_rows = dot(grad_residual_bf, out_full, ((1,), (1,))).astype(BF)
    grad_att = jnp.concatenate(
        exchange_z([grad_att_rows[:, m * head_cols : (m + 1) * head_cols] for m in range(nz)]),
        axis=0,
    ).reshape(group_rows, heads, HD)

    ffn_sum = None
    for m, block in enumerate(
        exchange_z(
            [
                jnp.concatenate(
                    [up_grad[m * units : (m + 1) * units], down_grad[m * units : (m + 1) * units]],
                    axis=0,
                ).astype(F32 if m == 0 else BF)
                for m in range(nz)
            ]
        )
    ):
        ffn_sum = block if ffn_sum is None else ffn_sum + block.astype(F32)
    ffn_sum = sum_beyond_plane(ffn_sum).astype(BF)
    ffn_stack = gather_plane(ffn_sum).reshape(sub, 2, units, width)
    ffn_perm = plane_permutation(1, sub, units)
    grad_w_up = dot(ffn_stack[:, 0].reshape(sub * units, width), ffn_perm, ((0,), (1,)))
    grad_w_down = dot(ffn_perm, ffn_stack[:, 1].reshape(sub * units, width), ((1,), (0,)))
    bias_sum = sum(exchange_z([bias_up_grad[m * units : (m + 1) * units][None] for m in range(nz)]))
    bias_stack = gather_plane(sum_beyond_plane(bias_sum)).reshape(1, sub * units)
    grad_b_up = lax.dot_general(
        bias_stack,
        ffn_perm.astype(F32),
        (((1,), (1,)), ((), ())),
        precision=lax.Precision.HIGHEST,
        preferred_element_type=F32,
    )[0]

    attended_perm = dot(attended_rows, out_perm, ((1,), (0,))).astype(BF)
    out_partial = dot(attended_perm, grad_residual_bf, ((0,), (0,)))
    out_plane = reduce_plane(out_partial)
    inner = head_cols // sub
    out_blocks = exchange_z(
        [
            out_plane[m * inner : (m + 1) * inner].astype(F32 if m == 0 else BF)
            for m in range(nz)
        ]
    )
    out_sum = out_blocks[0]
    for block in out_blocks[1:]:
        out_sum = out_sum + block.astype(F32)
    out_sum = sum_beyond_plane(out_sum).astype(BF)
    grad_w_out = dot(plane_permutation(1, sub, inner), gather_plane(out_sum), ((1,), (0,)))

    grad_queries, grad_keys, grad_values = attend_backward(
        queries, keys, values, attended, grad_att, log_total, allowed
    )
    grad_b_query = jnp.sum(grad_queries, axis=0).reshape(head_cols)
    grad_b_value = jnp.sum(grad_values, axis=0).reshape(head_cols)
    grad_joined = jnp.stack(
        [grad_queries.astype(BF), grad_keys.astype(BF), grad_values.astype(BF)], axis=2
    ).reshape(group_rows, 3 * head_cols)
    first_partial = dot(grad_joined, w_qkv, ((1,), (1,)))
    first_blocks = exchange_z(
        [
            first_partial[m * own : (m + 1) * own].astype(F32 if m == 0 else BF)
            for m in range(nz)
        ]
    )
    first_grad = first_blocks[0]
    for block in first_blocks[1:]:
        first_grad = first_grad + block.astype(F32)
    xhat_one, rstd_one = xhat_all[:own], rstd_all[:own]
    grad_input = grad_residual + norm_backward(first_grad, xhat_one, rstd_one, first_norm_gain)

    qkv_perm = plane_permutation(1, sub, 3 * head_cols // sub)
    joined_perm = dot(grad_joined, qkv_perm, ((1,), (0,))).astype(BF)
    qkv_sum = reduce_plane(dot(joined_perm, rows_one, ((0,), (0,))))
    qkv_stack = gather_plane(sum_beyond_plane(qkv_sum).astype(BF))
    grad_w_qkv = dot(qkv_stack, qkv_perm, ((0,), (1,)))

    early = sum_dp(
        sum_z(
            jnp.stack(
                [
                    jnp.sum(grad_final, axis=0),
                    jnp.sum(second_grad * xhat_two, axis=0),
                    jnp.sum(second_grad, axis=0),
                    jnp.sum(grad_residual, axis=0),
                ]
            )
        )
    )
    late = sum_dp(
        jnp.concatenate(
            [
                sum_z(
                    jnp.concatenate(
                        [
                            jnp.sum(first_partial * xhat_all, axis=0),
                            jnp.sum(first_partial, axis=0),
                        ]
                    )
                ),
                grad_b_query,
                grad_b_value,
            ]
        )[None]
    )[0]
    return (
        block_output,
        grad_input,
        grad_w_qkv,
        late[2 * width : 2 * width + head_cols],
        late[2 * width + head_cols :],
        grad_w_out,
        early[3],
        grad_w_up,
        grad_b_up,
        grad_w_down,
        early[0],
        late[:width],
        late[width : 2 * width],
        early[1],
        early[2],
    )


def solution(mesh):
    rows, cols = P(("dp", "tensor"), None), P(None, "tensor")
    vec, tall, full = P("tensor"), P("tensor", None), P()
    placed = (
        rows, P("dp", None), cols, vec, vec, tall, full, cols, vec, tall,
        full, full, full, full, full, rows,
    )
    given = (
        rows, rows, cols, vec, vec, tall, full, cols, vec, tall,
        full, full, full, full, full,
    )
    return jax.shard_map(local, mesh=mesh, in_specs=placed, out_specs=given, check_vma=False)
```

```python
import math

import jax
import jax.numpy as jnp
from jax import lax
from jax.experimental import pallas as pl
from jax.experimental.pallas import tpu as pltpu
from jax.sharding import PartitionSpec as P


HD = 64
GELU_COEF = 0.7978845608028654
GELU_CUBE = 0.044715
NORM_EPS = 1e-05
SCALE = 1.0 / math.sqrt(HD)
BF = jnp.bfloat16
F32 = jnp.float32
VEC = 8


def dot(left, right, left_dim, right_dim):
    return lax.dot_general(
        left, right, (((left_dim,), (right_dim,)), ((), ())), preferred_element_type=F32
    )


def swap(x, axis, mask):
    n = lax.axis_size(axis)
    return lax.ppermute(x, axis, [(i, i ^ mask) for i in range(n)])


def z_size():
    return lax.axis_size("tensor")


def plane_size():
    return min(8, lax.axis_size("dp"))


def send_z(blocks):
    return [swap(blocks[m - 1], "tensor", m) for m in range(1, z_size())]


def gather_z(x):
    return send_z([x] * (z_size() - 1))


def send_plane(blocks):
    return [swap(blocks[k - 1], "dp", 2 * k) for k in range(1, plane_size() // 2)]


def gather_plane(x):
    mine = join([x] + send_plane([x] * (plane_size() // 2 - 1)))
    return mine, swap(mine, "dp", 1)


def beyond(x):
    mask = plane_size()
    while mask < lax.axis_size("dp"):
        x = x.astype(F32)
        x = x + swap(x, "dp", mask)
        mask *= 2
    return x


def shape(rows, cols, dtype):
    return jax.ShapeDtypeStruct((rows, cols), dtype)


def size_of(x):
    return x.size * x.dtype.itemsize


def grant(args, outs, scratch, room):
    total = sum(size_of(a) for a in args) + sum(size_of(o) for o in outs)
    total += sum(math.prod(s.shape) * jnp.dtype(s.dtype).itemsize for s in scratch)
    return pltpu.CompilerParams(vmem_limit_bytes=total + room)


def call(body, outs, args, *, flops=0, scratch=(), smem=0, room=1 << 20):
    given = [pl.BlockSpec(memory_space=pltpu.SMEM)] * smem
    given += [pl.BlockSpec(memory_space=pltpu.VMEM)] * (len(args) - smem)
    single = not isinstance(outs, (list, tuple))
    outs = [outs] if single else list(outs)
    cost = pl.CostEstimate(
        flops=flops,
        bytes_accessed=sum(size_of(a) for a in args) + sum(size_of(o) for o in outs),
        transcendentals=0,
    )
    result = pl.pallas_call(
        body,
        out_shape=outs,
        in_specs=given,
        out_specs=[pl.BlockSpec(memory_space=pltpu.VMEM)] * len(outs),
        scratch_shapes=list(scratch),
        cost_estimate=cost,
        compiler_params=grant(args, outs, scratch, room),
    )(*args)
    return result[0] if single else result


def plane_index():
    return lax.rem(lax.axis_index("dp"), plane_size())


def one_hot(rows, cols, offset):
    row = lax.broadcasted_iota(jnp.int32, (rows, cols), 0)
    col = lax.broadcasted_iota(jnp.int32, (rows, cols), 1)
    return (col == row + offset).astype(BF)


def three(row):
    hi = row.astype(BF)
    rest = row - hi.astype(F32)
    mid = rest.astype(BF)
    low = (rest - mid.astype(F32)).astype(BF)
    index = lax.broadcasted_iota(jnp.int32, (VEC, row.shape[1]), 0)
    zero = jnp.zeros((VEC, row.shape[1]), F32)
    picked = jnp.where(index == 0, hi.astype(F32), zero)
    picked = jnp.where(index == 1, mid.astype(F32), picked)
    return jnp.where(index == 2, low.astype(F32), picked)


def two(vectors):
    hi = vectors.astype(BF).astype(F32)
    return hi, vectors - hi


def rows_of(vectors, width):
    index = lax.broadcasted_iota(jnp.int32, (VEC, width), 0)
    out = jnp.zeros((VEC, width), F32)
    for i, v in enumerate(vectors):
        out = jnp.where(index == i, v, out)
    return out


def standardize(values):
    centred = values - jnp.mean(values, axis=-1, keepdims=True)
    rstd = lax.rsqrt(jnp.mean(centred * centred, axis=-1, keepdims=True) + NORM_EPS)
    return centred * rstd, rstd


def norm_backward(grad_normed, xhat, rstd, gain):
    scaled = grad_normed * gain
    inner = jnp.mean(scaled * xhat, axis=-1, keepdims=True)
    return rstd * (scaled - jnp.mean(scaled, axis=-1, keepdims=True) - xhat * inner)


def join(blocks):
    rows, cols = blocks[0].shape

    def body(*refs):
        for i, ref in enumerate(refs[:-1]):
            refs[-1][i * rows : (i + 1) * rows] = ref[...]

    return call(body, shape(rows * len(blocks), cols, blocks[0].dtype), blocks)


def prepare_rows(block_input, w_out):
    own, width = block_input.shape
    cols = w_out.shape[0]
    inner = cols // plane_size()

    def body(x_ref, w_ref, o_ref):
        part = dot(one_hot(inner, cols, plane_index() * inner), w_ref[...], 1, 0)
        o_ref[:own] = x_ref[...]
        o_ref[own:] = part.astype(BF)

    return call(body, shape(own + inner, width, BF), [block_input, w_out])


def prepare_weights(w_up, w_down, b_up):
    hidden, width = w_down.shape
    units = hidden // plane_size()
    padded = -(-units // 128) * 128

    def body(up_ref, down_ref, bias_ref, o_ref):
        offset = plane_index() * units
        pick = one_hot(units, hidden, offset)
        o_ref[:units] = dot(pick, up_ref[...], 1, 1).astype(BF)
        o_ref[units : 2 * units] = dot(pick, down_ref[...], 1, 0).astype(BF)
        row = lax.broadcasted_iota(jnp.int32, (padded, hidden), 0)
        wide = jnp.where(row < units, one_hot(padded, hidden, offset).astype(F32), 0.0).astype(BF)
        bias = dot(three(bias_ref[...]).astype(BF), wide, 1, 1)
        o_ref[2 * units :, :padded] = bias.astype(BF)
        o_ref[2 * units :, padded:] = jnp.zeros((VEC, width - padded), BF)

    return call(
        body, shape(2 * units + VEC, width, BF), [w_up, w_down, b_up[None]],
        flops=4 * units * hidden * width,
    )


def prepare_cotangent(lengths, cotangent):
    own, width = cotangent.shape

    def body(len_ref, cot_ref, out_ref):
        total = jnp.int32(0)
        for i in range(len_ref.shape[1]):
            total = total + len_ref[0, i]
        slot = lax.axis_index("tensor") * own + lax.broadcasted_iota(jnp.int32, (own, width), 0)
        cot = cot_ref[...].astype(F32)
        out_ref[...] = jnp.where(slot < total, cot, cot * 0.0).astype(BF)

    return call(body, shape(own, width, BF), [lengths, cotangent], smem=1)


def prepare_out(blocks, own, inner):
    width = blocks[0].shape[1]

    def body(*refs):
        parts = [ref[own : own + inner].astype(F32) for ref in refs[:-1]]
        refs[-1][...] = jnp.concatenate(parts, axis=0).astype(BF)

    return call(body, shape(len(blocks) * inner, width, BF), list(blocks))


def allowed_pairs(len_ref, own, nz):
    t = lax.axis_index("tensor")
    n = own * nz

    def slots(index):
        out = jnp.zeros(index.shape, jnp.int32)
        for m in range(nz):
            inside = (index >= m * own) & (index < (m + 1) * own)
            out = jnp.where(inside, index - m * own + (t ^ m) * own, out)
        return out

    query = slots(lax.broadcasted_iota(jnp.int32, (1, n), 1))
    key = slots(lax.broadcasted_iota(jnp.int32, (n, 1), 0))
    start = jnp.zeros((1, n), jnp.int32)
    end = jnp.int32(0)
    for i in range(len_ref.shape[1]):
        end = end + len_ref[0, i]
        start = jnp.where(query >= end, end, start)
    return (key <= query) & (key >= start)


def attention_forward(lengths, blocks, own, w_t, b_query, b_value, gain, bias):
    nz = len(blocks)
    n = own * nz
    width = w_t.shape[1]
    cols = w_t.shape[0]
    heads = cols // (3 * HD)

    def body(len_ref, *refs):
        xs, refs = refs[:nz], refs[nz:]
        w_ref, bq_ref, bv_ref, g_ref, b_ref = refs[:5]
        att_refs, (qkv_ref, rows_ref, log_ref) = refs[5 : 5 + nz], refs[5 + nz :]
        for m in range(nz):
            xhat, _ = standardize(xs[m][:own].astype(F32))
            rows_ref[m * own : (m + 1) * own] = (xhat * g_ref[...] + b_ref[...]).astype(BF)
        joined = dot(w_ref[...], rows_ref[...], 1, 1)
        ones = jnp.ones((VEC, n), BF)
        bias_q = dot(three(bq_ref[...]).astype(BF), ones, 0, 0)
        bias_v = dot(three(bv_ref[...]).astype(BF), ones, 0, 0)
        allowed = allowed_pairs(len_ref, own, nz)
        log_ref[...] = jnp.zeros(log_ref.shape, F32)
        for h in range(heads):
            base = h * 3 * HD
            q = (joined[base : base + HD] + bias_q[h * HD : (h + 1) * HD]).astype(BF)
            k = joined[base + HD : base + 2 * HD].astype(BF)
            v = (joined[base + 2 * HD : base + 3 * HD] + bias_v[h * HD : (h + 1) * HD]).astype(BF)
            qkv_ref[base : base + HD] = q
            qkv_ref[base + HD : base + 2 * HD] = k
            qkv_ref[base + 2 * HD : base + 3 * HD] = v
            scores = jnp.where(allowed, dot(k, q, 0, 0) * SCALE, -jnp.inf)
            top = jnp.max(scores, axis=0, keepdims=True)
            log_total = top + jnp.log(jnp.sum(jnp.exp(scores - top), axis=0, keepdims=True))
            log_ref[h : h + 1] = log_total
            probs = jnp.exp(scores - log_total).astype(BF)
            out = dot(v, probs, 1, 0).astype(BF)
            for m in range(nz):
                att_refs[m][h * HD : (h + 1) * HD] = out[:, m * own : (m + 1) * own]

    outs = [shape(heads * HD, own, BF)] * nz
    outs += [shape(cols, n, BF), shape(n, width, BF), shape(VEC, n, F32)]
    out = call(
        body, outs,
        [lengths, *blocks, w_t, b_query[None], b_value[None], gain[None], bias[None]],
        flops=2 * n * width * cols + 4 * heads * n * n * HD, smem=1, room=8 << 20,
    )
    return out[:nz], *out[nz:]


def place_out(mine, other, inner, nz):
    sub = plane_size()
    width = mine.shape[1]
    rows = mine.shape[0] // (sub // 2)
    cols = inner * sub

    def body(mine_ref, other_ref, o_ref, acc):
        p = plane_index()
        for core, ref in enumerate((mine_ref, other_ref)):
            for k in range(sub // 2):
                part = ref[k * rows : (k + 1) * rows].astype(F32)
                j = p ^ (2 * k + core)
                for m in range(nz):
                    at = pl.multiple_of(m * cols + j * inner, 8)
                    acc[pl.ds(at, inner)] = part[m * inner : (m + 1) * inner]
        o_ref[...] = acc[...].astype(BF)

    return call(
        body, shape(nz * cols, width, BF), [mine, other],
        scratch=[pltpu.VMEM((nz * cols, width), F32)],
    )


def middle(att, out_full, block_input, b_out, gain, bias):
    own, width = block_input.shape
    nz = len(att)

    def body(*refs):
        w_ref, x_ref, bo_ref, g_ref, b_ref, res_ref, n_ref = refs[nz:]
        cat = jnp.concatenate([r[...] for r in refs[:nz]], axis=0)
        res = x_ref[...].astype(F32) + dot(cat, w_ref[...], 0, 0) + bo_ref[...]
        res_ref[...] = res
        xhat, _ = standardize(res)
        n_ref[...] = (xhat * g_ref[...] + b_ref[...]).astype(BF)

    return call(
        body, [shape(own, width, F32), shape(own, width, BF)],
        [*att, out_full, block_input, b_out[None], gain[None], bias[None]],
        flops=2 * own * width * width,
    )


def grid_call(body, steps, args, specs, outs, out_specs, scratch, flops):
    cost = pl.CostEstimate(
        flops=flops,
        bytes_accessed=sum(size_of(a) for a in args) + sum(size_of(o) for o in outs),
        transcendentals=0,
    )
    return pl.pallas_call(
        body, grid=(steps,), in_specs=specs, out_specs=out_specs, out_shape=outs,
        scratch_shapes=scratch, cost_estimate=cost,
        compiler_params=grant(args, outs, scratch, 4 << 20),
    )(*args)


def stepped(rows, cols):
    return pl.BlockSpec((rows, cols), lambda i: (i, 0))


def fixed(rows, cols):
    return pl.BlockSpec((rows, cols), lambda i: (0, 0))


def feed_forward(mine, other, mine_cot, other_cot, weights, own):
    width = mine.shape[1]
    steps = mine.shape[0] // own
    nz = len(weights)
    units = (weights[0].shape[0] - VEC) // 2
    padded = -(-units // 128) * 128
    hidden = nz * units
    cot_rows = mine_cot.shape[0] // steps

    def body(*refs):
        x0, x1, c0, c1 = refs[:4]
        w_refs = refs[4 : 4 + nz]
        keep, send, act_ref, pre_ref, bg_ref, up, down, bias_ref = refs[4 + nz :]
        step = pl.program_id(0)

        @pl.when(step == 0)
        def _():
            total = jnp.zeros((VEC, hidden), F32)
            for m in range(nz):
                up[m * units : (m + 1) * units] = w_refs[m][:units]
                down[m * units : (m + 1) * units] = w_refs[m][units : 2 * units]
                place = one_hot(padded, hidden, m * units)
                total = total + dot(w_refs[m][2 * units :, :padded], place, 1, 0)
            bias_ref[...] = jnp.broadcast_to(jnp.sum(total, axis=0, keepdims=True), (VEC, hidden))
            bg_ref[...] = jnp.zeros(bg_ref.shape, F32)

        rows = jnp.concatenate([x0[...], x1[...]], axis=0)
        cot = jnp.concatenate([c0[:own], c1[:own]], axis=0)
        values = dot(rows, up[...], 1, 1) + bias_ref[0:1]
        squared = values * values
        tangent = jnp.tanh(GELU_COEF * (values + GELU_CUBE * squared * values))
        half = 0.5 * (1.0 + tangent)
        act_ref[...] = (values * half).astype(BF)
        slope = half + 0.5 * values * (1.0 - tangent * tangent) * GELU_COEF * (
            1.0 + 3.0 * GELU_CUBE * squared
        )
        grad = dot(cot, down[...], 1, 1) * slope
        bg_ref[...] += jnp.broadcast_to(jnp.sum(grad, axis=0, keepdims=True), (VEC, hidden))
        grad = grad.astype(BF)
        pre_ref[...] = grad
        back = dot(grad, up[...], 1, 0)
        keep[...] = back[:own]
        send[...] = back[own:].astype(BF)

    n = 2 * steps * own
    return grid_call(
        body, steps, [mine, other, mine_cot, other_cot, *weights],
        [stepped(own, width)] * 2 + [stepped(cot_rows, width)] * 2
        + [fixed(*weights[0].shape)] * nz,
        [shape(n // 2, width, F32), shape(n // 2, width, BF), shape(n, hidden, BF),
         shape(n, hidden, BF), shape(VEC, hidden, F32)],
        [stepped(own, width)] * 2 + [stepped(2 * own, hidden)] * 2 + [fixed(VEC, hidden)],
        [pltpu.VMEM((hidden, width), BF), pltpu.VMEM((hidden, width), BF),
         pltpu.VMEM((VEC, hidden), F32)],
        6 * n * hidden * width,
    )


def feed_forward_weights(mine, other, mine_cot, other_cot, weights, act, pre, bias_grad, own):
    width = mine.shape[1]
    steps = mine.shape[0] // own
    nz = len(weights)
    units = (weights[0].shape[0] - VEC) // 2
    padded = -(-units // 128) * 128
    hidden = nz * units
    cot_rows = mine_cot.shape[0] // steps

    def body(*refs):
        x0, x1, c0, c1, act_ref, pre_ref, bg_ref = refs[:7]
        w_refs = refs[7 : 7 + nz]
        keep, send = refs[7 + nz : 9 + nz]
        packs = refs[9 + nz : 9 + 2 * nz]
        up_sum, down_sum, down = refs[9 + 2 * nz :]
        step = pl.program_id(0)

        @pl.when(step == 0)
        def _():
            for m in range(nz):
                down[m * units : (m + 1) * units] = w_refs[m][units : 2 * units]
            up_sum[...] = jnp.zeros(up_sum.shape, F32)
            down_sum[...] = jnp.zeros(down_sum.shape, F32)

        rows = jnp.concatenate([x0[...], x1[...]], axis=0)
        cot = jnp.concatenate([c0[:own], c1[:own]], axis=0)
        up_sum[...] += dot(pre_ref[...], rows, 0, 0)
        down_sum[...] += dot(act_ref[...], cot, 0, 0)
        out = dot(act_ref[...], down[...], 1, 0)
        keep[...] = out[:own]
        send[...] = out[own:].astype(BF)

        @pl.when(step == steps - 1)
        def _():
            bias_rows = three(bg_ref[0:1]).astype(BF)
            for m in range(nz):
                kind = packs[m].dtype
                part = slice(m * units, (m + 1) * units)
                packs[m][:units] = up_sum[part].astype(kind)
                packs[m][units : 2 * units] = down_sum[part].astype(kind)
                row = lax.broadcasted_iota(jnp.int32, (padded, hidden), 0)
                place = one_hot(padded, hidden, m * units).astype(F32)
                place = jnp.where(row < units, place, 0.0).astype(BF)
                packs[m][2 * units :, :padded] = dot(bias_rows, place, 1, 1).astype(kind)
                packs[m][2 * units :, padded:] = jnp.zeros((VEC, width - padded), kind)

    n = 2 * steps * own
    outs = [shape(n // 2, width, F32), shape(n // 2, width, BF)]
    outs += [shape(2 * units + VEC, width, F32 if m == 0 else BF) for m in range(nz)]
    out = grid_call(
        body, steps, [mine, other, mine_cot, other_cot, act, pre, bias_grad, *weights],
        [stepped(own, width)] * 2 + [stepped(cot_rows, width)] * 2
        + [stepped(2 * own, hidden)] * 2 + [fixed(VEC, hidden)] + [fixed(*weights[0].shape)] * nz,
        outs,
        [stepped(own, width)] * 2 + [fixed(2 * units + VEC, width)] * nz,
        [pltpu.VMEM((hidden, width), F32), pltpu.VMEM((hidden, width), F32),
         pltpu.VMEM((hidden, width), BF)],
        6 * n * hidden * width,
    )
    return out[0], out[1], out[2:]


def fold(keep, got, vec_at=None):
    blocks = plane_size() // 2
    rows = keep.shape[0] // blocks
    width = keep.shape[1]

    def body(keep_ref, got_ref, *outs):
        for k in range(blocks):
            part = slice(k * rows, (k + 1) * rows)
            total = keep_ref[part] + got_ref[part].astype(F32)
            if vec_at is not None:
                hi, low = two(total[vec_at : vec_at + VEC] + total[vec_at + VEC : vec_at + 2 * VEC])
                pieces = [total[:vec_at], hi, low]
                if vec_at + 2 * VEC < rows:
                    pieces.append(total[vec_at + 2 * VEC :])
                total = jnp.concatenate(pieces, axis=0)
            outs[k][...] = total.astype(outs[k].dtype)

    outs = [shape(rows, width, F32 if k == 0 else BF) for k in range(blocks)]
    return call(body, outs, [keep, got])


def total_of(refs):
    total = refs[0][...].astype(F32)
    for ref in refs[1:]:
        total = total + ref[...].astype(F32)
    return total


def second_backward(parts, residual, cot_rows, gain, out_full, nz):
    own, width = residual.shape
    cols = out_full.shape[0] // nz
    count = len(parts)

    def body(*refs):
        res_ref, cot_ref, g_ref, w_ref = refs[count : count + 4]
        grad_ref, bf_ref, vec_ref = refs[count + 4 : count + 7]
        outs = refs[count + 7 :]
        grad = total_of(refs[:count])
        xhat, rstd = standardize(res_ref[...])
        cot = cot_ref[...].astype(F32)
        grad_res = cot + norm_backward(grad, xhat, rstd, g_ref[...])
        grad_ref[...] = grad_res
        low = grad_res.astype(BF)
        bf_ref[...] = low
        for m in range(nz):
            outs[m][...] = dot(w_ref[m * cols : (m + 1) * cols], low, 1, 1).astype(BF)
        sums = [jnp.sum(v, axis=0, keepdims=True) for v in (cot, grad * xhat, grad, grad_res)]
        vec_ref[...] = rows_of(sums, width)

    out = call(
        body,
        [shape(own, width, F32), shape(own, width, BF), shape(VEC, width, F32)]
        + [shape(cols, own, BF)] * nz,
        [*parts, residual, cot_rows, gain[None], out_full],
        flops=2 * own * width * width,
    )
    return out[0], out[1], out[2], out[3:]


def out_gradient(att, grad_res_bf, mlp_keep, mlp_send, vec):
    sub, nz = plane_size(), len(att)
    cols, own = att[0].shape
    width = vec.shape[1]
    inner = cols // sub
    grad_rows = nz * inner
    rows = grad_rows + own + 2 * VEC
    blocks = sub // 2

    def body(*refs):
        g_ref, keep_in, send_in, vec_ref, keep, send, acc = refs[nz:]
        for m in range(nz):
            acc[m * cols : (m + 1) * cols] = dot(refs[m][...], g_ref[...], 1, 0)
        p = plane_index()
        hi, low = two(vec_ref[...])
        for core, ref in enumerate((keep, send)):
            for k in range(blocks):
                j = p ^ (2 * k + core)
                part = jnp.concatenate(
                    [
                        acc[pl.ds(pl.multiple_of(m * cols + j * inner, 8), inner)]
                        for m in range(nz)
                    ],
                    axis=0,
                )
                at = k * rows
                ref[at : at + grad_rows] = part.astype(ref.dtype)
                source = keep_in if core == 0 else send_in
                ref[at + grad_rows : at + grad_rows + own] = source[k * own : (k + 1) * own]
                ref[at + grad_rows + own : at + rows] = jnp.concatenate([hi, low], axis=0).astype(
                    ref.dtype
                )

    return call(
        body, [shape(blocks * rows, width, F32), shape(blocks * rows, width, BF)],
        [*att, grad_res_bf, mlp_keep, mlp_send, vec],
        flops=2 * own * width * width,
        scratch=[pltpu.VMEM((nz * cols, width), F32)],
    )


def block_result(parts, residual, b_down, late, lengths, nz):
    own, width = residual.shape
    count = len(parts)
    grad_rows = parts[0].shape[0] - own - 2 * VEC
    inner = grad_rows // nz

    def body(len_ref, *refs):
        res_ref, b_ref, late_ref, out_ref = refs[count : count + 4]
        packs = refs[count + 4 :]
        total = total_of(refs[:count])
        length = jnp.int32(0)
        for i in range(len_ref.shape[1]):
            length = length + len_ref[0, i]
        slot = lax.axis_index("tensor") * own + lax.broadcasted_iota(jnp.int32, (own, width), 0)
        final = res_ref[...] + total[grad_rows : grad_rows + own] + b_ref[...]
        out_ref[...] = jnp.where(slot < length, final, final * 0.0).astype(BF)
        at = grad_rows + own
        vec = total[at : at + VEC] + total[at + VEC : at + 2 * VEC]
        index = lax.broadcasted_iota(jnp.int32, (VEC, width), 0)
        for i in range(2):
            vec = jnp.where(index == 4 + i, late_ref[i : i + 1], vec)
        hi, low = two(vec)
        for m in range(nz):
            pack = jnp.concatenate([total[m * inner : (m + 1) * inner], hi, low], axis=0)
            packs[m][...] = pack.astype(packs[m].dtype)

    outs = [shape(own, width, BF)]
    outs += [shape(inner + 2 * VEC, width, F32 if m == 0 else BF) for m in range(nz)]
    out = call(body, outs, [lengths, *parts, residual, b_down[None], late], smem=1)
    return out[0], out[1:]


def weight_sums(ffn, out):
    count = len(ffn)
    rows, width = ffn[0].shape
    inner = out[0].shape[0] - 2 * VEC

    def body(*refs):
        pack_ref, vec_ref = refs[2 * count :]
        total = total_of(refs[:count])
        bias = jnp.sum(total[rows - VEC :], axis=0, keepdims=True)
        other = total_of(refs[count : 2 * count])
        vec_ref[...] = other[inner : inner + VEC] + other[inner + VEC :]
        pack_ref[...] = jnp.concatenate(
            [total[: rows - VEC], three(bias), other[:inner]], axis=0
        ).astype(BF)

    return call(body, [shape(rows + inner, width, BF), shape(VEC, width, F32)], [*ffn, *out])


def attention_backward(lengths, qkv, logs, att, grad_att, blocks, w_t, own):
    nz = len(blocks)
    cols, n = qkv.shape
    width = w_t.shape[1]
    heads = cols // (3 * HD)

    def body(len_ref, *refs):
        qkv_ref, log_ref = refs[:2]
        att_refs, ga_refs, xs = (refs[2 + i * nz : 2 + (i + 1) * nz] for i in range(3))
        w_ref = refs[2 + 3 * nz]
        outs = refs[3 + 3 * nz : 3 + 4 * nz]
        joined_ref, vec_ref, delta_rows = refs[3 + 4 * nz :]
        allowed = allowed_pairs(len_ref, own, nz)
        ga_all = jnp.concatenate([r[...] for r in ga_refs], axis=1)
        att_all = jnp.concatenate([r[...] for r in att_refs], axis=1)
        prod = ga_all.astype(F32) * att_all.astype(F32)
        for h in range(heads):
            base = h * 3 * HD
            q, k, v = (qkv_ref[base + i * HD : base + (i + 1) * HD] for i in range(3))
            ga = ga_all[h * HD : (h + 1) * HD]
            scores = jnp.where(allowed, dot(k, q, 0, 0) * SCALE, -jnp.inf)
            probs = jnp.exp(scores - log_ref[h : h + 1])
            grad_v = dot(ga, probs.astype(BF), 1, 1)
            delta = jnp.sum(prod[h * HD : (h + 1) * HD], axis=0, keepdims=True)
            grad_s = (probs * (dot(v, ga, 0, 0) - delta) * SCALE).astype(BF)
            grad_q = dot(k, grad_s, 1, 0)
            grad_k = dot(q, grad_s, 1, 1)
            joined_ref[base : base + HD] = grad_q.astype(BF)
            joined_ref[base + HD : base + 2 * HD] = grad_k.astype(BF)
            joined_ref[base + 2 * HD : base + 3 * HD] = grad_v.astype(BF)
            delta_rows[h * HD : (h + 1) * HD] = grad_q
            delta_rows[(heads + h) * HD : (heads + h + 1) * HD] = grad_v
        biases = lax.dot_general(
            jnp.ones((VEC, n), F32), delta_rows[...], (((1,), (1,)), ((), ())),
            precision=lax.Precision.HIGHEST, preferred_element_type=F32,
        )
        gain_sum = jnp.zeros((1, width), F32)
        bias_sum = jnp.zeros((1, width), F32)
        for m in range(nz):
            part = dot(joined_ref[:, m * own : (m + 1) * own], w_ref[...], 0, 0)
            outs[m][...] = part.astype(outs[m].dtype)
            xhat, _ = standardize(xs[m][:own].astype(F32))
            gain_sum = gain_sum + jnp.sum(part * xhat, axis=0, keepdims=True)
            bias_sum = bias_sum + jnp.sum(part, axis=0, keepdims=True)
        vec_ref[...] = rows_of([gain_sum, bias_sum], width)
        vec_ref[2:3, : 2 * heads * HD] = biases[0:1]

    outs = [shape(own, width, F32 if m == 0 else BF) for m in range(nz)]
    outs += [shape(cols, n, BF), shape(VEC, width, F32)]
    out = call(
        body, outs, [lengths, qkv, logs, *att, *grad_att, *blocks, w_t], smem=1,
        flops=2 * n * width * cols + 10 * heads * n * n * HD,
        scratch=[pltpu.VMEM((2 * heads * HD, n), F32)], room=12 << 20,
    )
    return out[:nz], out[nz], out[nz + 1]


def joined_gradient(joined, rows_one, vec):
    cols, n = joined.shape
    width = rows_one.shape[1]
    sub = plane_size()
    inner = cols // sub
    blocks = sub // 2
    rows = -(-(inner + 2 * VEC) // 16) * 16
    rest = rows - inner - 2 * VEC

    def body(g_ref, x_ref, vec_ref, keep, send, acc):
        acc[...] = dot(g_ref[...], x_ref[...], 1, 0)
        p = plane_index()
        hi, low = two(vec_ref[...])
        tail = [hi, low] + ([jnp.zeros((rest, width), F32)] if rest else [])
        for core, ref in enumerate((keep, send)):
            for k in range(blocks):
                j = p ^ (2 * k + core)
                part = acc[pl.ds(pl.multiple_of(j * inner, 8), inner)]
                ref[k * rows : (k + 1) * rows] = jnp.concatenate([part, *tail], axis=0).astype(
                    ref.dtype
                )

    return call(
        body, [shape(blocks * rows, width, F32), shape(blocks * rows, width, BF)],
        [joined, rows_one, vec], flops=2 * cols * n * width,
        scratch=[pltpu.VMEM((cols, width), F32)],
    )


def joined_sums(parts, inner):
    width = parts[0].shape[1]
    count = len(parts)

    def body(*refs):
        total = total_of(refs[:count])
        refs[count][...] = total[:inner].astype(BF)
        refs[count + 1][...] = total[inner : inner + VEC] + total[inner + VEC : inner + 2 * VEC]

    return call(body, [shape(inner, width, BF), shape(VEC, width, F32)], list(parts))


def first_backward(parts, block_input, grad_res, gain):
    own, width = grad_res.shape
    count = len(parts)

    def body(*refs):
        x_ref, r_ref, g_ref, out_ref = refs[count:]
        grad = total_of(refs[:count])
        xhat, rstd = standardize(x_ref[...].astype(F32))
        out_ref[...] = r_ref[...] + norm_backward(grad, xhat, rstd, g_ref[...])

    return call(body, shape(own, width, F32), [*parts, block_input, grad_res, gain[None]])


def assemble_weights(mine, other, units, inner):
    sub = plane_size()
    width = mine.shape[1]
    rows = mine.shape[0] // (sub // 2)
    hidden, cols = sub * units, sub * inner
    padded = -(-units // 128) * 128

    def body(mine_ref, other_ref, up_ref, down_ref, bias_ref, out_ref, acc):
        p = plane_index()
        bias = jnp.zeros((VEC, hidden), F32)
        for core, ref in enumerate((mine_ref, other_ref)):
            for k in range(sub // 2):
                j = p ^ (2 * k + core)
                at = pl.multiple_of(j * units, 8)
                part = ref[k * rows : (k + 1) * rows].astype(F32)
                acc[pl.ds(at, units)] = part[:units]
                down_ref[pl.ds(at, units)] = part[units : 2 * units]
                place = one_hot(padded, hidden, at)
                row = lax.broadcasted_iota(jnp.int32, (padded, hidden), 0)
                place = jnp.where(row < units, place.astype(F32), 0.0).astype(BF)
                tail = part[2 * units : 2 * units + VEC, :padded].astype(BF)
                bias = bias + dot(tail, place, 1, 0)
                out_ref[pl.ds(pl.multiple_of(j * inner, 8), inner)] = part[2 * units + VEC :]
        bias_ref[...] = jnp.broadcast_to(jnp.sum(bias, axis=0, keepdims=True), (VEC, hidden))
        up_ref[...] = jnp.transpose(acc[...])

    return call(
        body,
        [shape(width, hidden, F32), shape(hidden, width, F32), shape(VEC, hidden, F32),
         shape(cols, width, F32)],
        [mine, other], scratch=[pltpu.VMEM((hidden, width), F32)],
    )


def assemble_joined(mine, other):
    sub = plane_size()
    width = mine.shape[1]
    inner = mine.shape[0] // (sub // 2)

    def body(mine_ref, other_ref, out_ref):
        p = plane_index()
        for core, ref in enumerate((mine_ref, other_ref)):
            whole = ref[...].astype(F32)
            for k in range(sub // 2):
                j = p ^ (2 * k + core)
                out_ref[pl.ds(pl.multiple_of(j * inner, 8), inner)] = whole[
                    k * inner : (k + 1) * inner
                ]

    return call(body, shape(sub * inner, width, F32), [mine, other])


def local(
    block_input,
    seq_lengths,
    w_qkv,
    b_query,
    b_value,
    w_out,
    b_out,
    w_up,
    b_up,
    w_down,
    b_down,
    first_norm_gain,
    first_norm_bias,
    second_norm_gain,
    second_norm_bias,
    cotangent,
):
    own, _ = block_input.shape
    nz, sub = z_size(), plane_size()
    cols = w_out.shape[0]
    inner = cols // sub
    units = w_down.shape[0] // sub
    w_t = w_qkv.T

    row_pack = prepare_rows(block_input, w_out)
    row_blocks = [row_pack] + gather_z(row_pack)
    cot = prepare_cotangent(seq_lengths, cotangent)
    cot_mine, cot_other = gather_plane(cot)
    weight_pack = prepare_weights(w_up, w_down, b_up)
    out_mine, out_other = gather_plane(prepare_out(row_blocks, own, inner))

    att_sent, qkv, rows_one, logs = attention_forward(
        seq_lengths, row_blocks, own, w_t, b_query, b_value, first_norm_gain, first_norm_bias
    )
    att = [att_sent[0]] + send_z(att_sent[1:])
    weights = [weight_pack] + gather_z(weight_pack)
    out_full = place_out(out_mine, out_other, inner, nz)
    residual, normed_two = middle(
        att, out_full, block_input, b_out, second_norm_gain, second_norm_bias
    )
    mine, other = gather_plane(normed_two)

    keep, send, act, pre, bias_grad = feed_forward(
        mine, other, cot_mine, cot_other, weights, own
    )
    got = swap(send, "dp", 1)
    mlp_keep, mlp_send, ffn_packs = feed_forward_weights(
        mine, other, cot_mine, cot_other, weights, act, pre, bias_grad, own
    )
    folded = fold(keep, got)
    grad_res, grad_res_bf, early, grad_att_sent = second_backward(
        [folded[0]] + send_plane(folded[1:]), residual, cot, second_norm_gain, out_full, nz
    )
    grad_att = [grad_att_sent[0]] + send_z(grad_att_sent[1:])

    first_parts, joined, late = attention_backward(
        seq_lengths, qkv, logs, att_sent, grad_att, row_blocks, w_t, own
    )
    first_got = send_z(first_parts[1:])
    grad_input = first_backward(
        [first_parts[0]] + first_got, block_input, grad_res, first_norm_gain
    )

    joined_keep, joined_send = joined_gradient(joined, rows_one, late)
    joined_inner = joined.shape[0] // sub
    joined_folded = fold(joined_keep, swap(joined_send, "dp", 1), joined_inner)
    joined_sum, late_sum = joined_sums(
        [joined_folded[0]] + send_plane(joined_folded[1:]), joined_inner
    )
    grad_w_qkv = assemble_joined(*gather_plane(beyond(joined_sum).astype(BF))).T
    bias_sum = beyond(late_sum)[2]

    ffn_got = send_z(ffn_packs[1:])
    out_keep, out_send = out_gradient(att, grad_res_bf, mlp_keep, mlp_send, early)
    out_folded = fold(out_keep, swap(out_send, "dp", 1), nz * inner + own)
    block_output, out_packs = block_result(
        [out_folded[0]] + send_plane(out_folded[1:]), residual, b_down, late_sum, seq_lengths, nz
    )
    out_got = send_z(out_packs[1:])
    weight_pack_sum, early_sum = weight_sums(
        [beyond(x) for x in [ffn_packs[0], *ffn_got]], [beyond(x) for x in [out_packs[0], *out_got]]
    )
    grad_w_up, grad_w_down, grad_b_up, grad_w_out = assemble_weights(
        *gather_plane(weight_pack_sum), units, inner
    )

    return (
        block_output,
        grad_input,
        grad_w_qkv,
        bias_sum[:cols],
        bias_sum[cols : 2 * cols],
        grad_w_out,
        early_sum[3],
        grad_w_up,
        grad_b_up[0],
        grad_w_down,
        early_sum[0],
        early_sum[4],
        early_sum[5],
        early_sum[1],
        early_sum[2],
    )


def solution(mesh):
    rows, cols = P(("dp", "tensor"), None), P(None, "tensor")
    vec, tall, full = P("tensor"), P("tensor", None), P()
    placed = (
        rows, P("dp", None), cols, vec, vec, tall, full, cols, vec, tall,
        full, full, full, full, full, rows,
    )
    given = (
        rows, rows, cols, vec, vec, tall, full, cols, vec, tall,
        full, full, full, full, full,
    )

    return jax.shard_map(local, mesh=mesh, in_specs=placed, out_specs=given, check_vma=False)
```

```python
import math

import jax
import jax.numpy as jnp
from jax import lax
from jax.experimental import pallas as pl
from jax.experimental.pallas import tpu as pltpu
from jax.sharding import PartitionSpec as P


HD = 64
GELU_COEF = 0.7978845608028654
GELU_CUBE = 0.044715
NORM_EPS = 1e-05
SCALE = 1.0 / math.sqrt(HD)
BF = jnp.bfloat16
F32 = jnp.float32
VEC = 8


def dot(left, right, left_dim, right_dim):
    return lax.dot_general(
        left, right, (((left_dim,), (right_dim,)), ((), ())), preferred_element_type=F32
    )


def swap(x, axis, mask):
    n = lax.axis_size(axis)
    return lax.ppermute(x, axis, [(i, i ^ mask) for i in range(n)])


def z_size():
    return lax.axis_size("tensor")


def plane_size():
    return min(8, lax.axis_size("dp"))


def send_z(blocks):
    return [swap(blocks[m - 1], "tensor", m) for m in range(1, z_size())]


def gather_z(x):
    return send_z([x] * (z_size() - 1))


def send_plane(blocks):
    return [swap(blocks[k - 1], "dp", 2 * k) for k in range(1, plane_size() // 2)]


def gather_plane(x):
    mine = join([x] + send_plane([x] * (plane_size() // 2 - 1)))
    return mine, swap(mine, "dp", 1)


def beyond(x):
    mask = plane_size()
    while mask < lax.axis_size("dp"):
        x = x.astype(F32)
        x = x + swap(x, "dp", mask)
        mask *= 2
    return x


def shape(rows, cols, dtype):
    return jax.ShapeDtypeStruct((rows, cols), dtype)


def size_of(x):
    return x.size * x.dtype.itemsize


def grant(args, outs, scratch, room):
    total = sum(size_of(a) for a in args) + sum(size_of(o) for o in outs)
    total += sum(math.prod(s.shape) * jnp.dtype(s.dtype).itemsize for s in scratch)
    return pltpu.CompilerParams(vmem_limit_bytes=total + room)


def call(body, outs, args, *, flops=0, scratch=(), smem=0, room=1 << 20):
    given = [pl.BlockSpec(memory_space=pltpu.SMEM)] * smem
    given += [pl.BlockSpec(memory_space=pltpu.VMEM)] * (len(args) - smem)
    single = not isinstance(outs, (list, tuple))
    outs = [outs] if single else list(outs)
    cost = pl.CostEstimate(
        flops=flops,
        bytes_accessed=sum(size_of(a) for a in args) + sum(size_of(o) for o in outs),
        transcendentals=0,
    )
    result = pl.pallas_call(
        body,
        out_shape=outs,
        in_specs=given,
        out_specs=[pl.BlockSpec(memory_space=pltpu.VMEM)] * len(outs),
        scratch_shapes=list(scratch),
        cost_estimate=cost,
        compiler_params=grant(args, outs, scratch, room),
    )(*args)
    return result[0] if single else result


def plane_index():
    return lax.rem(lax.axis_index("dp"), plane_size())


def one_hot(rows, cols, offset):
    row = lax.broadcasted_iota(jnp.int32, (rows, cols), 0)
    col = lax.broadcasted_iota(jnp.int32, (rows, cols), 1)
    return (col == row + offset).astype(BF)


def three(row):
    hi = row.astype(BF)
    rest = row - hi.astype(F32)
    mid = rest.astype(BF)
    low = (rest - mid.astype(F32)).astype(BF)
    index = lax.broadcasted_iota(jnp.int32, (VEC, row.shape[1]), 0)
    zero = jnp.zeros((VEC, row.shape[1]), F32)
    picked = jnp.where(index == 0, hi.astype(F32), zero)
    picked = jnp.where(index == 1, mid.astype(F32), picked)
    return jnp.where(index == 2, low.astype(F32), picked)


def two(vectors):
    hi = vectors.astype(BF).astype(F32)
    return hi, vectors - hi


def rows_of(vectors, width):
    index = lax.broadcasted_iota(jnp.int32, (VEC, width), 0)
    out = jnp.zeros((VEC, width), F32)
    for i, v in enumerate(vectors):
        out = jnp.where(index == i, v, out)
    return out


def standardize(values):
    centred = values - jnp.mean(values, axis=-1, keepdims=True)
    rstd = lax.rsqrt(jnp.mean(centred * centred, axis=-1, keepdims=True) + NORM_EPS)
    return centred * rstd, rstd


def norm_backward(grad_normed, xhat, rstd, gain):
    scaled = grad_normed * gain
    inner = jnp.mean(scaled * xhat, axis=-1, keepdims=True)
    return rstd * (scaled - jnp.mean(scaled, axis=-1, keepdims=True) - xhat * inner)


def join(blocks):
    rows, cols = blocks[0].shape

    def body(*refs):
        for i, ref in enumerate(refs[:-1]):
            refs[-1][i * rows : (i + 1) * rows] = ref[...]

    return call(body, shape(rows * len(blocks), cols, blocks[0].dtype), blocks)


def prepare_slice(w_out):
    cols, width = w_out.shape
    inner = cols // plane_size()

    def body(w_ref, o_ref):
        pick = one_hot(inner, cols, plane_index() * inner)
        o_ref[...] = dot(pick, w_ref[...], 1, 0).astype(BF)

    return call(body, shape(inner, width, BF), [w_out])


def first_cut(units):
    return units * 2 // 3 // 16 * 16


def prepare_weights(w_up, w_down, b_up):
    hidden, width = w_down.shape
    units = hidden // plane_size()
    padded = -(-units // 128) * 128
    cut = first_cut(units)

    def body(up_ref, down_ref, bias_ref, a_ref, b_ref):
        offset = plane_index() * units
        pick = one_hot(units, hidden, offset)
        up = dot(pick, up_ref[...], 1, 1).astype(BF)
        a_ref[...] = up[:cut]
        b_ref[: units - cut] = up[cut:]
        at = 2 * units - cut
        b_ref[units - cut : at] = dot(pick, down_ref[...], 1, 0).astype(BF)
        row = lax.broadcasted_iota(jnp.int32, (padded, hidden), 0)
        wide = jnp.where(row < units, one_hot(padded, hidden, offset).astype(F32), 0.0).astype(BF)
        bias = dot(three(bias_ref[...]).astype(BF), wide, 1, 1)
        b_ref[at:, :padded] = bias.astype(BF)
        b_ref[at:, padded:] = jnp.zeros((VEC, width - padded), BF)

    return call(
        body, [shape(cut, width, BF), shape(2 * units - cut + VEC, width, BF)],
        [w_up, w_down, b_up[None]], flops=4 * units * hidden * width,
    )


def prepare_cotangent(lengths, cotangent):
    own, width = cotangent.shape

    def body(len_ref, cot_ref, out_ref):
        total = jnp.int32(0)
        for i in range(len_ref.shape[1]):
            total = total + len_ref[0, i]
        slot = lax.axis_index("tensor") * own + lax.broadcasted_iota(jnp.int32, (own, width), 0)
        cot = cot_ref[...].astype(F32)
        out_ref[...] = jnp.where(slot < total, cot, cot * 0.0).astype(BF)

    return call(body, shape(own, width, BF), [lengths, cotangent], smem=1)


def prepare_out(blocks):
    inner, width = blocks[0].shape

    def body(*refs):
        parts = [ref[...].astype(F32) for ref in refs[:-1]]
        refs[-1][...] = jnp.concatenate(parts, axis=0).astype(BF)

    return call(body, shape(len(blocks) * inner, width, BF), list(blocks))


def allowed_pairs(len_ref, own, nz):
    t = lax.axis_index("tensor")
    n = own * nz

    def slots(index):
        out = jnp.zeros(index.shape, jnp.int32)
        for m in range(nz):
            inside = (index >= m * own) & (index < (m + 1) * own)
            out = jnp.where(inside, index - m * own + (t ^ m) * own, out)
        return out

    query = slots(lax.broadcasted_iota(jnp.int32, (1, n), 1))
    key = slots(lax.broadcasted_iota(jnp.int32, (n, 1), 0))
    start = jnp.zeros((1, n), jnp.int32)
    end = jnp.int32(0)
    for i in range(len_ref.shape[1]):
        end = end + len_ref[0, i]
        start = jnp.where(query >= end, end, start)
    return (key <= query) & (key >= start)


def attention_forward(lengths, blocks, own, w_t, b_query, b_value, gain, bias):
    nz = len(blocks)
    n = own * nz
    width = w_t.shape[1]
    cols = w_t.shape[0]
    heads = cols // (3 * HD)

    def body(len_ref, *refs):
        xs, refs = refs[:nz], refs[nz:]
        w_ref, bq_ref, bv_ref, g_ref, b_ref = refs[:5]
        att_refs, (qkv_ref, rows_ref, log_ref) = refs[5 : 5 + nz], refs[5 + nz :]
        for m in range(nz):
            xhat, _ = standardize(xs[m][:own].astype(F32))
            rows_ref[m * own : (m + 1) * own] = (xhat * g_ref[...] + b_ref[...]).astype(BF)
        joined = dot(w_ref[...], rows_ref[...], 1, 1)
        ones = jnp.ones((VEC, n), BF)
        bias_q = dot(three(bq_ref[...]).astype(BF), ones, 0, 0)
        bias_v = dot(three(bv_ref[...]).astype(BF), ones, 0, 0)
        allowed = allowed_pairs(len_ref, own, nz)
        log_ref[...] = jnp.zeros(log_ref.shape, F32)
        for h in range(heads):
            base = h * 3 * HD
            q = (joined[base : base + HD] + bias_q[h * HD : (h + 1) * HD]).astype(BF)
            k = joined[base + HD : base + 2 * HD].astype(BF)
            v = (joined[base + 2 * HD : base + 3 * HD] + bias_v[h * HD : (h + 1) * HD]).astype(BF)
            qkv_ref[base : base + HD] = q
            qkv_ref[base + HD : base + 2 * HD] = k
            qkv_ref[base + 2 * HD : base + 3 * HD] = v
            scores = jnp.where(allowed, dot(k, q, 0, 0) * SCALE, -jnp.inf)
            top = jnp.max(scores, axis=0, keepdims=True)
            log_total = top + jnp.log(jnp.sum(jnp.exp(scores - top), axis=0, keepdims=True))
            log_ref[h : h + 1] = log_total
            probs = jnp.exp(scores - log_total).astype(BF)
            out = dot(v, probs, 1, 0).astype(BF)
            for m in range(nz):
                att_refs[m][h * HD : (h + 1) * HD] = out[:, m * own : (m + 1) * own]

    outs = [shape(heads * HD, own, BF)] * nz
    outs += [shape(cols, n, BF), shape(n, width, BF), shape(VEC, n, F32)]
    out = call(
        body, outs,
        [lengths, *blocks, w_t, b_query[None], b_value[None], gain[None], bias[None]],
        flops=2 * n * width * cols + 4 * heads * n * n * HD, smem=1, room=8 << 20,
    )
    return out[:nz], *out[nz:]


def place_out(mine, other, inner, nz):
    sub = plane_size()
    width = mine.shape[1]
    rows = mine.shape[0] // (sub // 2)
    cols = inner * sub

    def body(mine_ref, other_ref, o_ref, acc):
        p = plane_index()
        for core, ref in enumerate((mine_ref, other_ref)):
            for k in range(sub // 2):
                part = ref[k * rows : (k + 1) * rows].astype(F32)
                j = p ^ (2 * k + core)
                for m in range(nz):
                    at = pl.multiple_of(m * cols + j * inner, 8)
                    acc[pl.ds(at, inner)] = part[m * inner : (m + 1) * inner]
        o_ref[...] = acc[...].astype(BF)

    return call(
        body, shape(nz * cols, width, BF), [mine, other],
        scratch=[pltpu.VMEM((nz * cols, width), F32)],
    )


def middle(att, out_full, block_input, b_out, gain, bias):
    own, width = block_input.shape
    nz = len(att)

    def body(*refs):
        w_ref, x_ref, bo_ref, g_ref, b_ref, res_ref, n_ref = refs[nz:]
        cat = jnp.concatenate([r[...] for r in refs[:nz]], axis=0)
        res = x_ref[...].astype(F32) + dot(cat, w_ref[...], 0, 0) + bo_ref[...]
        res_ref[...] = res
        xhat, _ = standardize(res)
        n_ref[...] = (xhat * g_ref[...] + b_ref[...]).astype(BF)

    return call(
        body, [shape(own, width, F32), shape(own, width, BF)],
        [*att, out_full, block_input, b_out[None], gain[None], bias[None]],
        flops=2 * own * width * width,
    )


def grid_call(body, steps, args, specs, outs, out_specs, scratch, flops):
    cost = pl.CostEstimate(
        flops=flops,
        bytes_accessed=sum(size_of(a) for a in args) + sum(size_of(o) for o in outs),
        transcendentals=0,
    )
    return pl.pallas_call(
        body, grid=(steps,), in_specs=specs, out_specs=out_specs, out_shape=outs,
        scratch_shapes=scratch, cost_estimate=cost,
        compiler_params=grant(args, outs, scratch, 4 << 20),
    )(*args)


def stepped(rows, cols):
    return pl.BlockSpec((rows, cols), lambda i: (i, 0))


def fixed(rows, cols):
    return pl.BlockSpec((rows, cols), lambda i: (0, 0))


def feed_forward(mine, other, mine_cot, other_cot, first, rest, own):
    width = mine.shape[1]
    steps = mine.shape[0] // own
    nz = len(first)
    cut = first[0].shape[0]
    units = (cut + rest[0].shape[0] - VEC) // 2
    padded = -(-units // 128) * 128
    hidden = nz * units

    def body(*refs):
        x0, x1, c0, c1 = refs[:4]
        a_refs, b_refs = refs[4 : 4 + nz], refs[4 + nz : 4 + 2 * nz]
        keep, send, act_ref, pre_ref, bg_ref, up, down, bias_ref = refs[4 + 2 * nz :]
        step = pl.program_id(0)

        @pl.when(step == 0)
        def _():
            total = jnp.zeros((VEC, hidden), F32)
            for m in range(nz):
                at = m * units
                up[at : at + cut] = a_refs[m][...]
                up[at + cut : at + units] = b_refs[m][: units - cut]
                down[at : at + units] = b_refs[m][units - cut : 2 * units - cut]
                place = one_hot(padded, hidden, at)
                total = total + dot(b_refs[m][2 * units - cut :, :padded], place, 1, 0)
            bias_ref[...] = jnp.broadcast_to(jnp.sum(total, axis=0, keepdims=True), (VEC, hidden))
            bg_ref[...] = jnp.zeros(bg_ref.shape, F32)

        rows = jnp.concatenate([x0[...], x1[...]], axis=0)
        cot = jnp.concatenate([c0[...], c1[...]], axis=0)
        values = dot(rows, up[...], 1, 1) + bias_ref[0:1]
        squared = values * values
        tangent = jnp.tanh(GELU_COEF * (values + GELU_CUBE * squared * values))
        half = 0.5 * (1.0 + tangent)
        act_ref[...] = (values * half).astype(BF)
        slope = half + 0.5 * values * (1.0 - tangent * tangent) * GELU_COEF * (
            1.0 + 3.0 * GELU_CUBE * squared
        )
        grad = dot(cot, down[...], 1, 1) * slope
        bg_ref[...] += jnp.broadcast_to(jnp.sum(grad, axis=0, keepdims=True), (VEC, hidden))
        grad = grad.astype(BF)
        pre_ref[...] = grad
        back = dot(grad, up[...], 1, 0)
        keep[...] = back[:own]
        send[...] = back[own:].astype(BF)

    n = 2 * steps * own
    return grid_call(
        body, steps, [mine, other, mine_cot, other_cot, *first, *rest],
        [stepped(own, width)] * 4 + [fixed(*first[0].shape)] * nz + [fixed(*rest[0].shape)] * nz,
        [shape(n // 2, width, F32), shape(n // 2, width, BF), shape(n, hidden, BF),
         shape(n, hidden, BF), shape(VEC, hidden, F32)],
        [stepped(own, width)] * 2 + [stepped(2 * own, hidden)] * 2 + [fixed(VEC, hidden)],
        [pltpu.VMEM((hidden, width), BF), pltpu.VMEM((hidden, width), BF),
         pltpu.VMEM((VEC, hidden), F32)],
        6 * n * hidden * width,
    )


def feed_forward_weights(mine, other, mine_cot, other_cot, rest, act, pre, bias_grad, own, units):
    width = mine.shape[1]
    steps = mine.shape[0] // own
    nz = len(rest)
    padded = -(-units // 128) * 128
    hidden = nz * units
    down_at = rest[0].shape[0] - VEC - units

    def body(*refs):
        x0, x1, c0, c1, act_ref, pre_ref, bg_ref = refs[:7]
        w_refs = refs[7 : 7 + nz]
        keep, send = refs[7 + nz : 9 + nz]
        downs, ups = refs[9 + nz : 9 + 2 * nz], refs[9 + 2 * nz : 9 + 3 * nz]
        up_sum, down_sum, down = refs[9 + 3 * nz :]
        step = pl.program_id(0)

        @pl.when(step == 0)
        def _():
            for m in range(nz):
                down[m * units : (m + 1) * units] = w_refs[m][down_at : down_at + units]
            up_sum[...] = jnp.zeros(up_sum.shape, F32)
            down_sum[...] = jnp.zeros(down_sum.shape, F32)

        rows = jnp.concatenate([x0[...], x1[...]], axis=0)
        cot = jnp.concatenate([c0[...], c1[...]], axis=0)
        up_sum[...] += dot(pre_ref[...], rows, 0, 0)
        down_sum[...] += dot(act_ref[...], cot, 0, 0)
        out = dot(act_ref[...], down[...], 1, 0)
        keep[...] = out[:own]
        send[...] = out[own:].astype(BF)

        @pl.when(step == steps - 1)
        def _():
            bias_rows = three(bg_ref[0:1]).astype(BF)
            for m in range(nz):
                kind = ups[m].dtype
                part = slice(m * units, (m + 1) * units)
                ups[m][:units] = up_sum[part].astype(kind)
                downs[m][...] = down_sum[part].astype(kind)
                row = lax.broadcasted_iota(jnp.int32, (padded, hidden), 0)
                place = one_hot(padded, hidden, m * units).astype(F32)
                place = jnp.where(row < units, place, 0.0).astype(BF)
                ups[m][units:, :padded] = dot(bias_rows, place, 1, 1).astype(kind)
                ups[m][units:, padded:] = jnp.zeros((VEC, width - padded), kind)

    n = 2 * steps * own
    outs = [shape(n // 2, width, F32), shape(n // 2, width, BF)]
    outs += [shape(units, width, F32 if m == 0 else BF) for m in range(nz)]
    outs += [shape(units + VEC, width, F32 if m == 0 else BF) for m in range(nz)]
    out = grid_call(
        body, steps, [mine, other, mine_cot, other_cot, act, pre, bias_grad, *rest],
        [stepped(own, width)] * 4 + [stepped(2 * own, hidden)] * 2 + [fixed(VEC, hidden)]
        + [fixed(*rest[0].shape)] * nz,
        outs,
        [stepped(own, width)] * 2 + [fixed(units, width)] * nz + [fixed(units + VEC, width)] * nz,
        [pltpu.VMEM((hidden, width), F32), pltpu.VMEM((hidden, width), F32),
         pltpu.VMEM((hidden, width), BF)],
        6 * n * hidden * width,
    )
    return out[0], out[1], out[2 : 2 + nz], out[2 + nz :]


def fold(keep, got, vec_at=None):
    blocks = plane_size() // 2
    rows = keep.shape[0] // blocks
    width = keep.shape[1]

    def body(keep_ref, got_ref, *outs):
        for k in range(blocks):
            part = slice(k * rows, (k + 1) * rows)
            total = keep_ref[part] + got_ref[part].astype(F32)
            if vec_at is not None:
                hi, low = two(total[vec_at : vec_at + VEC] + total[vec_at + VEC : vec_at + 2 * VEC])
                pieces = [total[:vec_at], hi, low]
                if vec_at + 2 * VEC < rows:
                    pieces.append(total[vec_at + 2 * VEC :])
                total = jnp.concatenate(pieces, axis=0)
            outs[k][...] = total.astype(outs[k].dtype)

    outs = [shape(rows, width, F32 if k == 0 else BF) for k in range(blocks)]
    return call(body, outs, [keep, got])


def total_of(refs):
    total = refs[0][...].astype(F32)
    for ref in refs[1:]:
        total = total + ref[...].astype(F32)
    return total


def second_backward(parts, residual, cot_rows, gain, out_full, nz):
    own, width = residual.shape
    cols = out_full.shape[0] // nz
    count = len(parts)

    def body(*refs):
        res_ref, cot_ref, g_ref, w_ref = refs[count : count + 4]
        grad_ref, bf_ref, vec_ref = refs[count + 4 : count + 7]
        outs = refs[count + 7 :]
        grad = total_of(refs[:count])
        xhat, rstd = standardize(res_ref[...])
        cot = cot_ref[...].astype(F32)
        grad_res = cot + norm_backward(grad, xhat, rstd, g_ref[...])
        grad_ref[...] = grad_res
        low = grad_res.astype(BF)
        bf_ref[...] = low
        for m in range(nz):
            outs[m][...] = dot(w_ref[m * cols : (m + 1) * cols], low, 1, 1).astype(BF)
        sums = [jnp.sum(v, axis=0, keepdims=True) for v in (cot, grad * xhat, grad, grad_res)]
        vec_ref[...] = rows_of(sums, width)

    out = call(
        body,
        [shape(own, width, F32), shape(own, width, BF), shape(VEC, width, F32)]
        + [shape(cols, own, BF)] * nz,
        [*parts, residual, cot_rows, gain[None], out_full],
        flops=2 * own * width * width,
    )
    return out[0], out[1], out[2], out[3:]


def out_gradient(att, grad_res_bf, vec):
    sub, nz = plane_size(), len(att)
    cols, own = att[0].shape
    width = vec.shape[1]
    inner = cols // sub
    grad_rows = nz * inner
    rows = grad_rows + 2 * VEC
    blocks = sub // 2

    def body(*refs):
        g_ref, vec_ref, keep, send, acc = refs[nz:]
        for m in range(nz):
            acc[m * cols : (m + 1) * cols] = dot(refs[m][...], g_ref[...], 1, 0)
        p = plane_index()
        hi, low = two(vec_ref[...])
        for core, ref in enumerate((keep, send)):
            for k in range(blocks):
                j = p ^ (2 * k + core)
                parts = [
                    acc[pl.ds(pl.multiple_of(m * cols + j * inner, 8), inner)] for m in range(nz)
                ]
                ref[k * rows : (k + 1) * rows] = jnp.concatenate([*parts, hi, low], axis=0).astype(
                    ref.dtype
                )

    return call(
        body, [shape(blocks * rows, width, F32), shape(blocks * rows, width, BF)],
        [*att, grad_res_bf, vec], flops=2 * own * width * width,
        scratch=[pltpu.VMEM((nz * cols, width), F32)],
    )


def block_result(parts, rows, residual, b_down, late, lengths, nz):
    own, width = residual.shape
    count = len(parts)
    at = parts[0].shape[0] - 2 * VEC
    inner = at // nz

    def body(len_ref, *refs):
        row_refs = refs[count : count + len(rows)]
        res_ref, b_ref, late_ref, out_ref = refs[count + len(rows) : count + len(rows) + 4]
        packs = refs[count + len(rows) + 4 :]
        length = jnp.int32(0)
        for i in range(len_ref.shape[1]):
            length = length + len_ref[0, i]
        slot = lax.axis_index("tensor") * own + lax.broadcasted_iota(jnp.int32, (own, width), 0)
        final = res_ref[...] + total_of(row_refs) + b_ref[...]
        out_ref[...] = jnp.where(slot < length, final, final * 0.0).astype(BF)
        total = total_of(refs[:count])
        vec = total[at : at + VEC] + total[at + VEC : at + 2 * VEC]
        index = lax.broadcasted_iota(jnp.int32, (VEC, width), 0)
        for i in range(2):
            vec = jnp.where(index == 4 + i, late_ref[i : i + 1], vec)
        hi, low = two(vec)
        for m in range(nz):
            pack = jnp.concatenate([total[m * inner : (m + 1) * inner], hi, low], axis=0)
            packs[m][...] = pack.astype(packs[m].dtype)

    outs = [shape(own, width, BF)]
    outs += [shape(inner + 2 * VEC, width, F32 if m == 0 else BF) for m in range(nz)]
    out = call(body, outs, [lengths, *parts, *rows, residual, b_down[None], late], smem=1)
    return out[0], out[1:]


def weight_sums(downs, ups):
    count = len(downs)
    units, width = downs[0].shape

    def body(*refs):
        up = total_of(refs[count : 2 * count])
        bias = jnp.sum(up[units:], axis=0, keepdims=True)
        refs[2 * count][...] = jnp.concatenate(
            [up[:units], total_of(refs[:count]), three(bias)], axis=0
        ).astype(BF)

    return call(body, shape(2 * units + VEC, width, BF), [*downs, *ups])


def attention_backward(lengths, qkv, logs, att, grad_att, blocks, w_t, own):
    nz = len(blocks)
    cols, n = qkv.shape
    width = w_t.shape[1]
    heads = cols // (3 * HD)

    def body(len_ref, *refs):
        qkv_ref, log_ref = refs[:2]
        att_refs, ga_refs, xs = (refs[2 + i * nz : 2 + (i + 1) * nz] for i in range(3))
        w_ref = refs[2 + 3 * nz]
        outs = refs[3 + 3 * nz : 3 + 4 * nz]
        joined_ref, vec_ref, delta_rows = refs[3 + 4 * nz :]
        allowed = allowed_pairs(len_ref, own, nz)
        ga_all = jnp.concatenate([r[...] for r in ga_refs], axis=1)
        att_all = jnp.concatenate([r[...] for r in att_refs], axis=1)
        prod = ga_all.astype(F32) * att_all.astype(F32)
        for h in range(heads):
            base = h * 3 * HD
            q, k, v = (qkv_ref[base + i * HD : base + (i + 1) * HD] for i in range(3))
            ga = ga_all[h * HD : (h + 1) * HD]
            scores = jnp.where(allowed, dot(k, q, 0, 0) * SCALE, -jnp.inf)
            probs = jnp.exp(scores - log_ref[h : h + 1])
            grad_v = dot(ga, probs.astype(BF), 1, 1)
            delta = jnp.sum(prod[h * HD : (h + 1) * HD], axis=0, keepdims=True)
            grad_s = (probs * (dot(v, ga, 0, 0) - delta) * SCALE).astype(BF)
            grad_q = dot(k, grad_s, 1, 0)
            grad_k = dot(q, grad_s, 1, 1)
            joined_ref[base : base + HD] = grad_q.astype(BF)
            joined_ref[base + HD : base + 2 * HD] = grad_k.astype(BF)
            joined_ref[base + 2 * HD : base + 3 * HD] = grad_v.astype(BF)
            delta_rows[h * HD : (h + 1) * HD] = grad_q
            delta_rows[(heads + h) * HD : (heads + h + 1) * HD] = grad_v
        biases = lax.dot_general(
            jnp.ones((VEC, n), F32), delta_rows[...], (((1,), (1,)), ((), ())),
            precision=lax.Precision.HIGHEST, preferred_element_type=F32,
        )
        gain_sum = jnp.zeros((1, width), F32)
        bias_sum = jnp.zeros((1, width), F32)
        for m in range(nz):
            part = dot(joined_ref[:, m * own : (m + 1) * own], w_ref[...], 0, 0)
            outs[m][...] = part.astype(outs[m].dtype)
            xhat, _ = standardize(xs[m][:own].astype(F32))
            gain_sum = gain_sum + jnp.sum(part * xhat, axis=0, keepdims=True)
            bias_sum = bias_sum + jnp.sum(part, axis=0, keepdims=True)
        vec_ref[...] = rows_of([gain_sum, bias_sum], width)
        vec_ref[2:3, : 2 * heads * HD] = biases[0:1]

    outs = [shape(own, width, F32 if m == 0 else BF) for m in range(nz)]
    outs += [shape(cols, n, BF), shape(VEC, width, F32)]
    out = call(
        body, outs, [lengths, qkv, logs, *att, *grad_att, *blocks, w_t], smem=1,
        flops=2 * n * width * cols + 10 * heads * n * n * HD,
        scratch=[pltpu.VMEM((2 * heads * HD, n), F32)], room=12 << 20,
    )
    return out[:nz], out[nz], out[nz + 1]


def joined_gradient(joined, rows_one, vec):
    cols, n = joined.shape
    width = rows_one.shape[1]
    sub = plane_size()
    inner = cols // sub
    blocks = sub // 2
    rows = -(-(inner + 2 * VEC) // 16) * 16
    rest = rows - inner - 2 * VEC

    def body(g_ref, x_ref, vec_ref, keep, send, acc):
        acc[...] = dot(g_ref[...], x_ref[...], 1, 0)
        p = plane_index()
        hi, low = two(vec_ref[...])
        tail = [hi, low] + ([jnp.zeros((rest, width), F32)] if rest else [])
        for core, ref in enumerate((keep, send)):
            for k in range(blocks):
                j = p ^ (2 * k + core)
                part = acc[pl.ds(pl.multiple_of(j * inner, 8), inner)]
                ref[k * rows : (k + 1) * rows] = jnp.concatenate([part, *tail], axis=0).astype(
                    ref.dtype
                )

    return call(
        body, [shape(blocks * rows, width, F32), shape(blocks * rows, width, BF)],
        [joined, rows_one, vec], flops=2 * cols * n * width,
        scratch=[pltpu.VMEM((cols, width), F32)],
    )


def joined_sums(parts, out, joined_rows):
    width = parts[0].shape[1]
    count = len(parts)
    inner = out[0].shape[0] - 2 * VEC

    def body(*refs):
        total = total_of(refs[:count])
        other = total_of(refs[count : count + len(out)])
        pack_ref, early_ref, late_ref = refs[count + len(out) :]
        vec = other[inner : inner + VEC] + other[inner + VEC :]
        early_ref[...] = vec
        hi, low = two(vec)
        late_ref[...] = (
            total[joined_rows : joined_rows + VEC] + total[joined_rows + VEC : joined_rows + 2 * VEC]
        )
        tail = rows_of([hi[4:5], hi[5:6], low[4:5], low[5:6]], width)
        pack_ref[...] = jnp.concatenate([total[:joined_rows], other[:inner], tail], axis=0).astype(
            BF
        )

    return call(
        body,
        [shape(joined_rows + inner + VEC, width, BF), shape(VEC, width, F32),
         shape(VEC, width, F32)],
        [*parts, *out],
    )


def first_backward(parts, block_input, grad_res, gain):
    own, width = grad_res.shape
    count = len(parts)

    def body(*refs):
        x_ref, r_ref, g_ref, out_ref = refs[count:]
        grad = total_of(refs[:count])
        xhat, rstd = standardize(x_ref[...].astype(F32))
        out_ref[...] = r_ref[...] + norm_backward(grad, xhat, rstd, g_ref[...])

    return call(body, shape(own, width, F32), [*parts, block_input, grad_res, gain[None]])


def assemble_weights(mine, other, units):
    sub = plane_size()
    width = mine.shape[1]
    rows = mine.shape[0] // (sub // 2)
    hidden = sub * units
    padded = -(-units // 128) * 128

    def body(mine_ref, other_ref, up_ref, down_ref, bias_ref, acc):
        p = plane_index()
        bias = jnp.zeros((VEC, hidden), F32)
        row = lax.broadcasted_iota(jnp.int32, (padded, hidden), 0)
        for core, ref in enumerate((mine_ref, other_ref)):
            for k in range(sub // 2):
                j = p ^ (2 * k + core)
                at = pl.multiple_of(j * units, 8)
                part = ref[k * rows : (k + 1) * rows].astype(F32)
                acc[pl.ds(at, units)] = part[:units]
                down_ref[pl.ds(at, units)] = part[units : 2 * units]
                place = jnp.where(row < units, one_hot(padded, hidden, at).astype(F32), 0.0)
                tail = part[2 * units :, :padded].astype(BF)
                bias = bias + dot(tail, place.astype(BF), 1, 0)
        bias_ref[...] = jnp.sum(bias, axis=0, keepdims=True)
        up_ref[...] = jnp.transpose(acc[...])

    return call(
        body,
        [shape(width, hidden, F32), shape(hidden, width, F32), shape(1, hidden, F32)],
        [mine, other], scratch=[pltpu.VMEM((hidden, width), F32)],
    )


def assemble_joined(mine, other, joined_rows, inner):
    sub = plane_size()
    width = mine.shape[1]
    rows = mine.shape[0] // (sub // 2)

    def body(mine_ref, other_ref, joined_ref, out_ref, vec_ref):
        p = plane_index()
        vec = jnp.zeros((VEC, width), F32)
        for core, ref in enumerate((mine_ref, other_ref)):
            whole = ref[...].astype(F32)
            for k in range(sub // 2):
                j = p ^ (2 * k + core)
                part = whole[k * rows : (k + 1) * rows]
                joined_ref[pl.ds(pl.multiple_of(j * joined_rows, 8), joined_rows)] = part[
                    :joined_rows
                ]
                out_ref[pl.ds(pl.multiple_of(j * inner, 8), inner)] = part[
                    joined_rows : joined_rows + inner
                ]
                vec = vec + part[joined_rows + inner :]
        vec_ref[...] = vec[0:2] + vec[2:4]

    return call(
        body,
        [shape(sub * joined_rows, width, F32), shape(sub * inner, width, F32),
         shape(2, width, F32)],
        [mine, other],
    )


def local(
    block_input,
    seq_lengths,
    w_qkv,
    b_query,
    b_value,
    w_out,
    b_out,
    w_up,
    b_up,
    w_down,
    b_down,
    first_norm_gain,
    first_norm_bias,
    second_norm_gain,
    second_norm_bias,
    cotangent,
):
    own, _ = block_input.shape
    nz, sub = z_size(), plane_size()
    cols = w_out.shape[0]
    inner = cols // sub
    units = w_down.shape[0] // sub
    w_t = w_qkv.T

    row_blocks = [block_input] + gather_z(block_input)
    out_slice = prepare_slice(w_out)
    out_slices = [out_slice] + gather_z(out_slice)
    cot = prepare_cotangent(seq_lengths, cotangent)
    cot_mine, cot_other = gather_plane(cot)
    weights_a, weights_b = prepare_weights(w_up, w_down, b_up)
    out_mine, out_other = gather_plane(prepare_out(out_slices))
    first = [weights_a] + gather_z(weights_a)

    att_sent, qkv, rows_one, logs = attention_forward(
        seq_lengths, row_blocks, own, w_t, b_query, b_value, first_norm_gain, first_norm_bias
    )
    att = [att_sent[0]] + send_z(att_sent[1:])
    rest = [weights_b] + gather_z(weights_b)
    out_full = place_out(out_mine, out_other, inner, nz)
    residual, normed_two = middle(
        att, out_full, block_input, b_out, second_norm_gain, second_norm_bias
    )
    mine, other = gather_plane(normed_two)

    keep, send, act, pre, bias_grad = feed_forward(
        mine, other, cot_mine, cot_other, first, rest, own
    )
    got = swap(send, "dp", 1)
    mlp_keep, mlp_send, downs, ups = feed_forward_weights(
        mine, other, cot_mine, cot_other, rest, act, pre, bias_grad, own, units
    )
    folded = fold(keep, got)
    mlp_folded = fold(mlp_keep, swap(mlp_send, "dp", 1))
    mlp_parts = [mlp_folded[0]] + send_plane(mlp_folded[1:])
    grad_res, grad_res_bf, early, grad_att_sent = second_backward(
        [folded[0]] + send_plane(folded[1:]), residual, cot, second_norm_gain, out_full, nz
    )
    grad_att = [grad_att_sent[0]] + send_z(grad_att_sent[1:])

    first_parts, joined, late = attention_backward(
        seq_lengths, qkv, logs, att_sent, grad_att, row_blocks, w_t, own
    )
    first_got = send_z(first_parts[1:])
    grad_input = first_backward(
        [first_parts[0]] + first_got, block_input, grad_res, first_norm_gain
    )

    joined_inner = joined.shape[0] // sub
    joined_keep, joined_send = joined_gradient(joined, rows_one, late)
    joined_folded = fold(joined_keep, swap(joined_send, "dp", 1), joined_inner)
    joined_parts = [joined_folded[0]] + send_plane(joined_folded[1:])
    out_keep, out_send = out_gradient(att, grad_res_bf, early)
    out_folded = fold(out_keep, swap(out_send, "dp", 1), nz * inner)
    block_output, out_packs = block_result(
        [out_folded[0]] + send_plane(out_folded[1:]),
        mlp_parts, residual, b_down, late, seq_lengths, nz,
    )
    out_parts = [out_packs[0]] + send_z(out_packs[1:])

    downs = [downs[0]] + send_z(downs[1:])
    ups = [ups[0]] + send_z(ups[1:])
    weight_pack = weight_sums([beyond(x) for x in downs], [beyond(x) for x in ups])
    grad_w_up, grad_w_down, grad_b_up = assemble_weights(*gather_plane(weight_pack), units)

    joined_pack, early_sum, late_sum = joined_sums(
        [beyond(x) for x in joined_parts], [beyond(x) for x in out_parts], joined_inner
    )
    grad_joined_t, grad_w_out, norm_sum = assemble_joined(
        *gather_plane(joined_pack), joined_inner, inner
    )
    grad_w_qkv = grad_joined_t.T
    return (
        block_output,
        grad_input,
        grad_w_qkv,
        late_sum[2, :cols],
        late_sum[2, cols : 2 * cols],
        grad_w_out,
        early_sum[3],
        grad_w_up,
        grad_b_up[0],
        grad_w_down,
        early_sum[0],
        norm_sum[0],
        norm_sum[1],
        early_sum[1],
        early_sum[2],
    )


def solution(mesh):
    rows, cols = P(("dp", "tensor"), None), P(None, "tensor")
    vec, tall, full = P("tensor"), P("tensor", None), P()
    placed = (
        rows, P("dp", None), cols, vec, vec, tall, full, cols, vec, tall,
        full, full, full, full, full, rows,
    )
    given = (
        rows, rows, cols, vec, vec, tall, full, cols, vec, tall,
        full, full, full, full, full,
    )

    return jax.shard_map(local, mesh=mesh, in_specs=placed, out_specs=given, check_vma=False)
```
